256 devices in a mesh: tower: 2 (over y_lo), blk: 32 (over z, y_hi, core), mp: 4 (over x).
Axes of the slice: x: 4, y: 4 (y_hi: 2, y_lo: 2; y = y_hi * 2 + y_lo), z: 8, core: 2. Of those that a mesh axis runs over, the one named last changes fastest.
Arguments:
- image_feats: bfloat16 [32768, 5120], P('blk', 'mp'), may hold values from -6 to 6
- text_feats: bfloat16 [32768, 1280], P('blk', 'mp'), may hold values from -6 to 6
- image_proj: bfloat16 [5120, 1024], P('mp'), may hold values from -0.05729924 to 0.05729924
- text_proj: bfloat16 [1280, 1024], P('mp'), may hold values from -0.11459848 to 0.11459848
- logit_scale: float32 [], replicated, may hold values from 30 to 300
- pairs: int32 [32, 1024], P('blk'), may hold values from 0 to 1023, as said below
Outputs:
- image_loss: float32 [32768], P('blk')
- text_loss: float32 [32768], P('blk')
The draws below stay inside these ranges and needn't reach their ends.
Inputs may be any that keep to these rules, and one draw needn't show every extreme that they name: Each row pairs[b] is a permutation of 0 to 1023: image b * 1024 + i is paired with caption b * 1024 + pairs[b, i].
All inputs are finite; a program needn't handle non-finite values.
Results may differ from the reference program's by a relative error of at most 0.0017.
Values may be sent and summed in bfloat16 or wider, within the bound.
A program may use at most 64 MiB of HBM per device.

```python
import jax
import jax.numpy as jnp
from jax import lax

WI = 5120
WT = 1280
EMB = 1024
ROWS = 1024
BATCH = 32768
N_BLK = 32


def projection_pair(key):
    image_weight = jnp.clip(jax.random.normal(jax.random.fold_in(key, 101), (WI, EMB), jnp.float32), -4.0, 4.0) * WI ** (-0.5)
    text_weight = jnp.clip(jax.random.normal(jax.random.fold_in(key, 102), (WT, EMB), jnp.float32), -4.0, 4.0) * WT ** (-0.5)
    return (image_weight.astype(jnp.bfloat16).astype(jnp.float32), text_weight.astype(jnp.bfloat16).astype(jnp.float32))


def pair_table(key):
    shard_keys = jax.random.split(jax.random.fold_in(key, 108), N_BLK)

    def permute(subkey):
        return jax.random.permutation(subkey, ROWS)
    return jax.vmap(permute)(shard_keys).astype(jnp.int32)


def caption_table(key):
    features = jnp.clip(jax.random.normal(jax.random.fold_in(key, 103), (BATCH, WT), jnp.float32), -6.0, 6.0)
    return features.astype(jnp.bfloat16).astype(jnp.float32)


def draw_pairs(key, part):
    return pair_table(key).astype(jnp.int32)


def draw_image_proj(key, part):
    return projection_pair(key)[0].astype(jnp.bfloat16)


def draw_text_proj(key, part):
    return projection_pair(key)[1].astype(jnp.bfloat16)


def draw_text_feats(key, part):
    return caption_table(key).astype(jnp.bfloat16)


def draw_logit_scale(key, part):
    return jax.random.uniform(jax.random.fold_in(key, 109), (), jnp.float32, 30.0, 100.0).astype(jnp.float32)


def draw_image_feats(key, part):
    noise_rows = jnp.clip(jax.random.normal(jax.random.fold_in(key, 106), (BATCH, WI), jnp.float32), -6.0, 6.0)
    return noise_rows.astype(jnp.bfloat16)


def setup_inputs(seed: int = 0) -> dict:
    splits = jax.random.split(jax.random.key(seed), 7)
    return {
        "image_feats": draw_image_feats(jax.random.fold_in(splits[6], 71), 0),
        "text_feats": draw_text_feats(jax.random.fold_in(splits[6], 71), 0),
        "image_proj": draw_image_proj(jax.random.fold_in(splits[6], 71), 0),
        "text_proj": draw_text_proj(jax.random.fold_in(splits[6], 71), 0),
        "logit_scale": draw_logit_scale(jax.random.fold_in(splits[6], 71), 0),
        "pairs": draw_pairs(jax.random.fold_in(splits[6], 71), 0),
    }


def embed_rows(features, weights, feature_width):
    values = features.astype(jnp.float32)
    row_mean = lax.optimization_barrier(jnp.sum(values, axis=1, keepdims=True)) / feature_width
    row_square = lax.optimization_barrier(jnp.sum(values * values, axis=1, keepdims=True)) / feature_width
    inverse = lax.rsqrt(row_square - row_mean * row_mean + 1e-06)
    normed = ((values - row_mean) * inverse).astype(jnp.bfloat16)
    projected = jnp.dot(normed.astype(jnp.float32), weights.astype(jnp.float32), preferred_element_type=jnp.float32)
    length = lax.rsqrt(lax.optimization_barrier(jnp.sum(projected * projected, axis=1, keepdims=True)) + 1e-06)
    return (projected * length).astype(jnp.bfloat16)

def reference(image_feats, text_feats, image_proj, text_proj, logit_scale, pairs):
    images = embed_rows(image_feats, image_proj, WI)
    captions = embed_rows(text_feats, text_proj, WT)
    shards = images.reshape(N_BLK, ROWS, EMB)

    def visit_shard(running, inputs):
        column_max, column_sum = running
        shard_rows, shard_pairs, shard_index = inputs
        scores = logit_scale * jnp.dot(shard_rows.astype(jnp.float32), captions.T.astype(jnp.float32), preferred_element_type=jnp.float32)
        row_max = lax.optimization_barrier(jnp.max(scores, axis=1))
        row_lse = row_max + jnp.log(lax.optimization_barrier(jnp.sum(jnp.exp(scores - row_max[:, None]), axis=1)))
        targets = (shard_index * ROWS + shard_pairs).astype(jnp.int32)
        positive = jnp.take_along_axis(scores, targets[:, None], axis=1)[:, 0]
        tile_max = lax.optimization_barrier(jnp.max(scores, axis=0))
        new_max = jnp.maximum(column_max, tile_max)
        column_sum = column_sum * jnp.exp(column_max - new_max) + lax.optimization_barrier(jnp.sum(jnp.exp(scores - new_max[None, :]), axis=0))
        return ((new_max, column_sum), (row_lse, positive))
    initial = (jnp.full((BATCH,), -jnp.inf, jnp.float32), jnp.zeros((BATCH,), jnp.float32))
    (column_max, column_sum), (row_lse, positive) = lax.scan(visit_shard, initial, (shards, pairs, jnp.arange(N_BLK, dtype=jnp.int32)))
    caption_lse = column_max + jnp.log(column_sum)
    targets = (jnp.arange(N_BLK, dtype=jnp.int32)[:, None] * ROWS + pairs).reshape(-1).astype(jnp.int32)
    caption_positive = jnp.zeros((BATCH,), jnp.float32).at[targets].set(positive.reshape(-1))
    return ((row_lse - positive).reshape(-1), caption_lse - caption_positive)
```

```python
import jax
import jax.numpy as jnp
from jax import lax
from jax.experimental import pallas as pl
from jax.experimental.pallas import tpu as pltpu
from jax.sharding import PartitionSpec as P

MESH = pl.DeviceIdType.MESH
F32 = jnp.float32
BF16 = jnp.bfloat16
ROWS = 1024
EMB = 1024
WIDTH = (5120, 1280)
LOCAL = (1280, 320)
PIECE = 128
HALF = 64
QUART = 32
NSEM = 160
LOW = -1e30


def wrap(value, count):
    return lax.rem(value + count, count)


def kernel(
    imf, txf, wim, wtx, scale_ref, pairs_ref, out_img, out_txt,
    xi, xt, wi, wt, mus, pf, pb, misc_send, misc_recv, relay, comb, fin, turn,
    img, txt, rmax, rsum, cmax, csum, rsend, rrecv, csend, crecv, fsend, frecv,
    lsem, ssem, rsem,
):
    tw = lax.axis_index("tower")
    blk = lax.axis_index("blk")
    x = lax.axis_index("mp")
    core = lax.rem(blk, 2)
    yh = lax.rem(blk // 2, 2)
    z = blk // 4
    y = yh * 2 + tw
    piece = tw * 4 + x

    def device(dx, dy, dz, dc):
        px = wrap(x + dx, 4)
        py = wrap(y + dy, 4)
        pz = wrap(z + dz, 8)
        pc = lax.rem(core + dc, 2)
        return {"tower": lax.rem(py, 2), "blk": (pz * 2 + py // 2) * 2 + pc, "mp": px}

    sent = []

    def send(src, dst, where):
        k = len(sent)
        copy = pltpu.make_async_remote_copy(
            src_ref=src, dst_ref=dst, send_sem=ssem.at[k], recv_sem=rsem.at[k],
            device_id=device(*where), device_id_type=MESH,
        )
        copy.start()
        sent.append(copy)
        return k

    def arrive(k, ref):
        pltpu.make_async_remote_copy(
            src_ref=ref, dst_ref=ref, send_sem=ssem.at[k], recv_sem=rsem.at[k],
            device_id=device(1, 0, 0, 0), device_id_type=MESH,
        ).wait_recv()

    half_rows = pl.ds(pl.multiple_of(tw * 512, 512), 512)
    loads = [
        pltpu.make_async_copy(imf.at[half_rows, :], xi, lsem.at[0]),
        pltpu.make_async_copy(wim, wi, lsem.at[1]),
        pltpu.make_async_copy(txf.at[half_rows, :], xt, lsem.at[2]),
        pltpu.make_async_copy(wtx, wt, lsem.at[3]),
    ]
    for load in loads:
        load.start()

    plane = [(dx, dy, 0, 0) for dy in range(4) for dx in range(4) if (dx, dy) != (0, 0)]
    column = [(0, 0, dz, dc) for dz in range(8) for dc in range(2) if (dz, dc) != (0, 0)]
    barrier = pltpu.get_barrier_semaphore()
    for where in plane + column:
        pl.semaphore_signal(barrier, inc=1, device_id=device(*where), device_id_type=MESH)

    lane = lax.broadcasted_iota(jnp.int32, (PIECE, PIECE), 1)

    def project(q, feats, weights):
        width = LOCAL[q]

        def rows_stats(d, carry):
            rows = pl.ds(pl.multiple_of(d * PIECE, PIECE), PIECE)
            values = feats[rows, :].astype(F32)
            first = jnp.sum(values, axis=1, keepdims=True)
            second = jnp.sum(values * values, axis=1, keepdims=True)
            mus[q, rows, :] = first / width
            flat = jnp.where(lane == 0, first, jnp.where(lane == 1, second, 0.0)).T
            misc_send[q, d, :, EMB : EMB + 128] = flat[0:1, :]
            misc_send[q, d, :, EMB + 128 : EMB + 256] = flat[1:2, :]
            return carry

        lax.fori_loop(0, 4, rows_stats, 0)

        def columns_step(n, carry):
            cols = pl.ds(pl.multiple_of(n * 256, 256), 256)
            block = weights[:, cols]
            total = jnp.dot(jnp.ones((8, width), BF16), block, preferred_element_type=F32)[0:1, :]
            part = jnp.dot(feats[...], block, preferred_element_type=F32) - mus[q] * total
            pf[q, :, cols] = part
            pb[q, :, cols] = part.astype(BF16)
            for d in range(4):
                misc_send[q, d, :, cols] = total
            return carry

        lax.fori_loop(0, 4, columns_step, 0)

    right, left, opposite = wrap(x + 1, 4), wrap(x + 3, 4), wrap(x + 2, 4)

    def part_rows(owner, start, count):
        return pl.ds(pl.multiple_of(owner * PIECE + start, HALF), count)

    def scatter_first(q):
        keys = {}
        keys["relay0"] = send(pb.at[q, part_rows(opposite, 0, HALF), :], relay.at[q, 0], (1, 0, 0, 0))
        keys["relay1"] = send(pb.at[q, part_rows(opposite, HALF, HALF), :], relay.at[q, 1], (3, 0, 0, 0))
        keys["fin0b"] = send(
            pb.at[q, part_rows(right, HALF, HALF), :], fin.at[q, 0, pl.ds(HALF, HALF), :], (1, 0, 0, 0)
        )
        keys["fin1a"] = send(
            pb.at[q, part_rows(left, 0, HALF), :], fin.at[q, 1, pl.ds(0, HALF), :], (3, 0, 0, 0)
        )
        keys["misc"] = [
            send(misc_send.at[q, wrap(x + d, 4)], misc_recv.at[q, x], (d, 0, 0, 0)) for d in (1, 3, 2)
        ]
        return keys

    def scatter_second(q, keys):
        arrive(keys["relay0"], relay.at[q, 0])
        comb[q, 0] = (pf[q, part_rows(right, 0, HALF), :] + relay[q, 0].astype(F32)).astype(BF16)
        keys["fin0a"] = send(comb.at[q, 0], fin.at[q, 0, pl.ds(0, HALF), :], (1, 0, 0, 0))
        arrive(keys["relay1"], relay.at[q, 1])
        comb[q, 1] = (pf[q, part_rows(left, HALF, HALF), :] + relay[q, 1].astype(F32)).astype(BF16)
        keys["fin1b"] = send(comb.at[q, 1], fin.at[q, 1, pl.ds(HALF, HALF), :], (3, 0, 0, 0))

    def finish(q, keys):
        for d, k in zip((1, 3, 2), keys["misc"]):
            arrive(k, misc_recv.at[q, wrap(x - d, 4)])
        misc_recv[q, x] = misc_send[q, x]
        turn[...] = jnp.zeros_like(turn)
        first = [misc_recv[q, s, :, EMB : EMB + 128] for s in range(4)]
        second = [misc_recv[q, s, :, EMB + 128 : EMB + 256] for s in range(4)]
        mean = (first[0] + first[1] + first[2] + first[3]) / WIDTH[q]
        square = (second[0] + second[1] + second[2] + second[3]) / WIDTH[q]
        turn[4:5, :] = lax.rsqrt(square - mean * mean + 1e-06)
        for s in range(4):
            turn[s : s + 1, :] = first[s] / LOCAL[q] - mean
        columns = turn[...].T
        arrive(keys["fin0b"], fin.at[q, 0, pl.ds(HALF, HALF), :])
        arrive(keys["fin1a"], fin.at[q, 1, pl.ds(0, HALF), :])
        arrive(keys["fin0a"], fin.at[q, 0, pl.ds(0, HALF), :])
        arrive(keys["fin1b"], fin.at[q, 1, pl.ds(HALF, HALF), :])
        total = pf[q, part_rows(x, 0, PIECE), :] + fin[q, 0].astype(F32) + fin[q, 1].astype(F32)
        for s in range(4):
            total = total + columns[:, s : s + 1] * misc_recv[q, s, :, 0:EMB]
        projected = total * columns[:, 4:5]
        length = lax.rsqrt(jnp.sum(projected * projected, axis=1, keepdims=True) + 1e-06)
        return (projected * length).astype(BF16)

    loads[0].wait()
    loads[1].wait()
    project(0, xi, wi)
    pl.semaphore_wait(barrier, len(plane) + len(column))
    keys0 = scatter_first(0)
    loads[2].wait()
    loads[3].wait()
    project(1, xt, wt)
    keys1 = scatter_first(1)
    rmax[...] = jnp.full(rmax.shape, LOW, F32)
    rsum[...] = jnp.zeros(rsum.shape, F32)
    cmax[...] = jnp.full(cmax.shape, LOW, F32)
    csum[...] = jnp.zeros(csum.shape, F32)
    scatter_second(0, keys0)
    scatter_second(1, keys1)

    def unit_a(dx, dy):
        return wrap(y + dy, 4), wrap(x + dx, 4)

    def unit_b(dx, dy):
        return 4 + wrap(x + dx, 4), wrap(y + dy, 4)

    def chunk(pair, start=0, count=HALF):
        unit, place = pair
        return img.at[unit, pl.ds(pl.multiple_of(place * HALF + start, QUART), count), :]

    MOVE = {"x": lambda s: (s, 0, 0, 0), "y": lambda s: (0, s, 0, 0)}

    def spread(axis, ref):
        return [send(ref, ref, MOVE[axis](1)), send(ref, ref, MOVE[axis](3))]

    def pass_on(axis, keys, lower, upper):
        arrive(keys[0], chunk(lower))
        low = send(chunk(lower, 0, QUART), chunk(lower, 0, QUART), MOVE[axis](1))
        arrive(keys[1], chunk(upper))
        high = send(chunk(upper, QUART, QUART), chunk(upper, QUART, QUART), MOVE[axis](3))
        return low, high

    def land(keys, far):
        arrive(keys[0], chunk(far, 0, QUART))
        arrive(keys[1], chunk(far, QUART, QUART))

    emb_img = finish(0, keys0)
    own_a, own_b = unit_a(0, 0), unit_b(0, 0)
    img[own_a[0], pl.ds(pl.multiple_of(own_a[1] * HALF, HALF), HALF), :] = emb_img[0:HALF]
    img[own_b[0], pl.ds(pl.multiple_of(own_b[1] * HALF, HALF), HALF), :] = emb_img[HALF:PIECE]
    a_x = spread("x", chunk(own_a))
    b_y = spread("y", chunk(own_b))
    a_y = {0: spread("y", chunk(own_a))}
    b_x = {0: spread("x", chunk(own_b))}

    def cap(dz, other=0, start=0, count=PIECE):
        place = lax.rem(core + other, 2) * PIECE
        return txt.at[wrap(z + dz, 8), pl.ds(pl.multiple_of(place + start, HALF), count), :]

    emb_txt = finish(1, keys1)
    txt[z, pl.ds(pl.multiple_of(core * PIECE, PIECE), PIECE), :] = emb_txt
    up = {1: send(cap(0), cap(0), (0, 0, 1, 0))}
    down = {1: send(cap(0), cap(0), (0, 0, 7, 0))}
    pair_keys = {0: send(cap(0), cap(0), (0, 0, 0, 1))}

    def captions_step(d):
        if d < 4:
            arrive(up[d], cap(-d))
            if d < 3:
                up[d + 1] = send(cap(-d), cap(-d), (0, 0, 1, 0))
            else:
                up[4] = send(cap(-3, 0, 0, HALF), cap(-3, 0, 0, HALF), (0, 0, 1, 0))
            pair_keys[-d] = send(cap(-d), cap(-d), (0, 0, 0, 1))
            arrive(down[d], cap(d))
            if d < 3:
                down[d + 1] = send(cap(d), cap(d), (0, 0, 7, 0))
            else:
                down[4] = send(cap(3, 0, HALF, HALF), cap(3, 0, HALF, HALF), (0, 0, 7, 0))
            pair_keys[d] = send(cap(d), cap(d), (0, 0, 0, 1))
        else:
            arrive(up[4], cap(4, 0, 0, HALF))
            arrive(down[4], cap(4, 0, HALF, HALF))
            pair_keys[4] = send(cap(4), cap(4), (0, 0, 0, 1))

    scale = scale_ref[0, 0]

    def signed(k):
        return ((k + 1) // 2) * (1 - 2 * lax.rem(k + 1, 2))

    def tile(j, k):
        kind = lax.rem(j, 2)
        unit = kind * 4 + wrap((1 - kind) * y + kind * x + signed(j // 2), 4)
        column_unit = wrap(z + signed(k), 8)
        scores = scale * lax.dot_general(
            img[unit], txt[column_unit], (((1,), (1,)), ((), ())), preferred_element_type=F32
        )
        top = jnp.max(scores, axis=1, keepdims=True)
        total = jnp.sum(jnp.exp(scores - top), axis=1, keepdims=True)
        old = rmax[unit]
        new = jnp.maximum(old, top)
        rsum[unit] = rsum[unit] * jnp.exp(old - new) + total * jnp.exp(top - new)
        rmax[unit] = new
        top = jnp.max(scores, axis=0, keepdims=True)
        total = jnp.sum(jnp.exp(scores - top), axis=0, keepdims=True)
        old = cmax[column_unit]
        new = jnp.maximum(old, top)
        csum[column_unit] = csum[column_unit] * jnp.exp(old - new) + total * jnp.exp(top - new)
        cmax[column_unit] = new

    def wave(j0, j1, k0, k1):
        span = k1 - k0

        def step(i, carry):
            tile(j0 + i // span, k0 + lax.rem(i, span))
            return carry

        lax.fori_loop(0, (j1 - j0) * span, step, 0)

    def sibling(dz):
        arrive(pair_keys[dz], cap(dz, 1))

    a_far, b_far = {}, {}
    a_x_far = pass_on("x", a_x, unit_a(-1, 0), unit_a(1, 0))
    b_y_far = pass_on("y", b_y, unit_b(0, -1), unit_b(0, 1))
    for s in (-1, 1):
        a_y[s] = spread("y", chunk(unit_a(s, 0)))
        b_x[s] = spread("x", chunk(unit_b(0, s)))
    a_far[0] = pass_on("y", a_y[0], unit_a(0, -1), unit_a(0, 1))
    b_far[0] = pass_on("x", b_x[0], unit_b(-1, 0), unit_b(1, 0))
    land(a_x_far, unit_a(2, 0))
    land(b_y_far, unit_b(0, 2))
    a_y[2] = spread("y", chunk(unit_a(2, 0)))
    b_x[2] = spread("x", chunk(unit_b(0, 2)))
    captions_step(1)
    sibling(0)
    wave(0, 2, 0, 1)
    for s in (-1, 1):
        a_far[s] = pass_on("y", a_y[s], unit_a(s, -1), unit_a(s, 1))
        b_far[s] = pass_on("x", b_x[s], unit_b(-1, s), unit_b(1, s))
    sibling(-1)
    sibling(1)
    wave(0, 2, 1, 3)
    captions_step(2)
    a_far[2] = pass_on("y", a_y[2], unit_a(2, -1), unit_a(2, 1))
    b_far[2] = pass_on("x", b_x[2], unit_b(-1, 2), unit_b(1, 2))
    wave(2, 6, 0, 3)
    sibling(-2)
    sibling(2)
    captions_step(3)
    wave(0, 6, 3, 5)

    sibling(-3)
    sibling(3)
    wave(0, 6, 5, 7)
    captions_step(4)
    for s in (0, -1, 1, 2):
        land(a_far[s], unit_a(s, 2))
        land(b_far[s], unit_b(2, s))
    own_caps = txt[z, pl.ds(pl.multiple_of(core * PIECE, PIECE), PIECE), :]
    turn[...] = jnp.zeros_like(turn)
    turn[0:8, :] = pairs_ref[...].astype(F32)
    partner = turn[...].T
    mine = (piece * PIECE + lane).astype(F32)
    caption_positive = jnp.zeros((1, PIECE), F32)
    image_positive = jnp.zeros((PIECE, PIECE), F32)
    for p in range(8):
        t, px = p // 4, p % 4
        rows = jnp.concatenate(
            [
                img[yh * 2 + t, px * HALF : (px + 1) * HALF, :],
                img[4 + px, pl.ds(pl.multiple_of((yh * 2 + t) * HALF, HALF), HALF), :],
            ],
            axis=0,
        )
        scores = scale * lax.dot_general(
            rows, own_caps, (((1,), (1,)), ((), ())), preferred_element_type=F32
        )
        picked = jnp.where(partner[:, p : p + 1] == mine, scores, 0.0)
        caption_positive = caption_positive + jnp.sum(picked, axis=0, keepdims=True)
        image_positive = jnp.where(lane == p, jnp.sum(picked, axis=1, keepdims=True), image_positive)
    image_positive = image_positive.T

    wave(6, 8, 0, 7)
    sibling(4)
    wave(0, 8, 7, 8)

    for u in range(8):
        logs = cmax[u] + jnp.log(csum[u])
        csend[2 * u] = logs[:, 0:PIECE]
        csend[2 * u + 1] = logs[:, PIECE : 2 * PIECE]
    me_column = z * 2 + core
    column_keys = []
    for where in column:
        target = wrap(z + where[2], 8) * 2 + lax.rem(core + where[3], 2)
        column_keys.append(send(csend.at[target], crecv.at[me_column], where))
    wide = lax.broadcasted_iota(jnp.int32, (256, PIECE), 1)
    logs = jnp.zeros((256, PIECE), F32)
    for u in range(8):
        logs = jnp.where(wide == u, rmax[u] + jnp.log(rsum[u]), logs)
    logs_low, logs_high = logs[0:PIECE].T, logs[PIECE:256].T
    parts = [logs_low, logs_high]

    def quarter(u, place):
        return parts[place // 2][u : u + 1, (place % 2) * HALF : (place % 2 + 1) * HALF]

    same = [(yh == 0).astype(F32), (yh == 1).astype(F32)]
    for py in range(4):
        for px in range(4):
            rsend[py * 4 + px, 0:1, :] = jnp.concatenate([quarter(py, px), quarter(4 + px, py)], axis=1)
            p = (py % 2) * 4 + px
            rsend[py * 4 + px, 1:2, :] = image_positive[p : p + 1, :] * same[py // 2]
    me_plane = y * 4 + x
    plane_keys = []
    for where in plane:
        target = wrap(y + where[1], 4) * 4 + wrap(x + where[0], 4)
        plane_keys.append(send(rsend.at[target], rrecv.at[me_plane], where))
    crecv[me_column] = csend[me_column]
    rrecv[me_plane] = rsend[me_plane]
    for where, k in zip(column, column_keys):
        source = wrap(z - where[2], 8) * 2 + lax.rem(core + where[3], 2)
        arrive(k, crecv.at[source])
    for where, k in zip(plane, plane_keys):
        source = wrap(y - where[1], 4) * 4 + wrap(x - where[0], 4)
        arrive(k, rrecv.at[source])

    def merge(rows):
        top = jnp.max(rows, axis=0)
        return top + jnp.log(jnp.sum(jnp.exp(rows - top[None]), axis=0))

    image_rows = rrecv[...]
    fsend[0:1, :] = merge(image_rows[:, 0:1, :]) - jnp.sum(image_rows[:, 1:2, :], axis=0)
    fsend[1:2, :] = merge(crecv[...]) - caption_positive
    shard = [(dx, dt) for dt in range(2) for dx in range(4) if (dx, dt) != (0, 0)]
    shard_keys = []
    step_y = [0, 1 - 2 * tw]
    for dx, dt in shard:
        shard_keys.append(send(fsend, frecv.at[piece], (dx, step_y[dt], 0, 0)))
    frecv[piece] = fsend[...]
    for (dx, dt), k in zip(shard, shard_keys):
        source = lax.rem(tw + dt, 2) * 4 + wrap(x - dx, 4)
        arrive(k, frecv.at[source])
    for p in range(8):
        out_img[p : p + 1, :] = frecv[p, 0:1, :]
        out_txt[p : p + 1, :] = frecv[p, 1:2, :]
    for copy in sent:
        copy.wait_send()


def on_device(image_feats, text_feats, image_proj, text_proj, logit_scale, pairs):
    vmem = pl.BlockSpec(memory_space=pltpu.VMEM)
    hbm = pl.BlockSpec(memory_space=pl.ANY)
    out = jax.ShapeDtypeStruct((8, 128), F32)
    image_loss, text_loss = pl.pallas_call(
        kernel,
        out_shape=(out, out),
        in_specs=[hbm, hbm, hbm, hbm, pl.BlockSpec(memory_space=pltpu.SMEM), vmem],
        out_specs=(vmem, vmem),
        scratch_shapes=[
            pltpu.VMEM((512, LOCAL[0]), BF16),
            pltpu.VMEM((512, LOCAL[1]), BF16),
            pltpu.VMEM((LOCAL[0], EMB), BF16),
            pltpu.VMEM((LOCAL[1], EMB), BF16),
            pltpu.VMEM((2, 512, 1), F32),
            pltpu.VMEM((2, 512, EMB), F32),
            pltpu.VMEM((2, 512, EMB), BF16),
            pltpu.VMEM((2, 4, 1, EMB + 256), F32),
            pltpu.VMEM((2, 4, 1, EMB + 256), F32),
            pltpu.VMEM((2, 2, HALF, EMB), BF16),
            pltpu.VMEM((2, 2, HALF, EMB), BF16),
            pltpu.VMEM((2, 2, PIECE, EMB), BF16),
            pltpu.VMEM((PIECE, PIECE), F32),
            pltpu.VMEM((8, 256, EMB), BF16),
            pltpu.VMEM((8, 256, EMB), BF16),
            pltpu.VMEM((8, 256, 1), F32),
            pltpu.VMEM((8, 256, 1), F32),
            pltpu.VMEM((8, 1, 256), F32),
            pltpu.VMEM((8, 1, 256), F32),
            pltpu.VMEM((16, 2, PIECE), F32),
            pltpu.VMEM((16, 2, PIECE), F32),
            pltpu.VMEM((16, 1, PIECE), F32),
            pltpu.VMEM((16, 1, PIECE), F32),
            pltpu.VMEM((2, PIECE), F32),
            pltpu.VMEM((8, 2, PIECE), F32),
            pltpu.SemaphoreType.DMA((4,)),
            pltpu.SemaphoreType.DMA((NSEM,)),
            pltpu.SemaphoreType.DMA((NSEM,)),
        ],
        compiler_params=pltpu.CompilerParams(
            collective_id=0, has_side_effects=True, vmem_limit_bytes=60 * 1024 * 1024
        ),
    )(
        image_feats, text_feats, image_proj, text_proj,
        logit_scale.reshape(1, 1), pairs.reshape(8, 128),
    )
    return (image_loss.reshape(ROWS), text_loss.reshape(ROWS))


def solution(mesh):
    return jax.shard_map(
        on_device,
        mesh=mesh,
        in_specs=(
            P("blk", "mp"),
            P("blk", "mp"),
            P("mp", None),
            P("mp", None),
            P(),
            P("blk", None),
        ),
        out_specs=(P("blk"), P("blk")),
        check_vma=False,
    )
```

```python
import jax
import jax.numpy as jnp
from jax import lax
from jax.experimental import pallas as pl
from jax.experimental.pallas import tpu as pltpu
from jax.sharding import PartitionSpec as P

MESH = pl.DeviceIdType.MESH
F32 = jnp.float32
BF16 = jnp.bfloat16
ROWS = 1024
EMB = 1024
WIDTH = (5120, 1280)
LOCAL = (1280, 320)
PIECE = 128
HALF = 64
QUART = 32
NSEM = 160
NA, NB = 80, 48
CUT_A, CUT_B = 48, 16
LOG2E = 1.4426950408889634
LN2 = 0.6931471805599453
LOW = -1e30


def wrap(value, count):
    return lax.rem(value + count, count)


def kernel(
    imf, txf, wim, wtx, scale_ref, pairs_ref, out,
    xi, xt, wi, wt, mus, pf, pb, misc_send, misc_recv, relay, comb, fin, turn, columns,
    img_a, img_b, txt, rmax_a, rsum_a, rmax_b, rsum_b, cmax, csum,
    rsend, rrecv, csend, crecv, fsend, frecv, lsem, ssem, rsem,
):
    tw = lax.axis_index("tower")
    blk = lax.axis_index("blk")
    x = lax.axis_index("mp")
    core = lax.rem(blk, 2)
    yh = lax.rem(blk // 2, 2)
    z = blk // 4
    y = yh * 2 + tw
    piece = tw * 4 + x

    def device(dx, dy, dz, dc):
        px = wrap(x + dx, 4)
        py = wrap(y + dy, 4)
        pz = wrap(z + dz, 8)
        pc = lax.rem(core + dc, 2)
        return {"tower": lax.rem(py, 2), "blk": (pz * 2 + py // 2) * 2 + pc, "mp": px}

    sent = []

    def send(src, dst, where):
        k = len(sent)
        copy = pltpu.make_async_remote_copy(
            src_ref=src, dst_ref=dst, send_sem=ssem.at[k], recv_sem=rsem.at[k],
            device_id=device(*where), device_id_type=MESH,
        )
        copy.start()
        sent.append(copy)
        return k

    def arrive(k, ref):
        pltpu.make_async_remote_copy(
            src_ref=ref, dst_ref=ref, send_sem=ssem.at[k], recv_sem=rsem.at[k],
            device_id=device(1, 0, 0, 0), device_id_type=MESH,
        ).wait_recv()

    half_rows = pl.ds(pl.multiple_of(tw * 512, 512), 512)
    loads = [
        pltpu.make_async_copy(imf.at[half_rows, :], xi, lsem.at[0]),
        pltpu.make_async_copy(wim, wi, lsem.at[1]),
        pltpu.make_async_copy(txf.at[:, half_rows], xt, lsem.at[2]),
        pltpu.make_async_copy(wtx, wt, lsem.at[3]),
    ]
    for load in loads:
        load.start()

    plane = [(dx, dy, 0, 0) for dy in range(4) for dx in range(4) if (dx, dy) != (0, 0)]
    column = [(0, 0, dz, dc) for dz in range(8) for dc in range(2) if (dz, dc) != (0, 0)]
    barrier = pltpu.get_barrier_semaphore()
    for where in plane + column:
        pl.semaphore_signal(barrier, inc=1, device_id=device(*where), device_id_type=MESH)

    lane = lax.broadcasted_iota(jnp.int32, (PIECE, PIECE), 1)

    def project(q, feats, weights):
        width = LOCAL[q]

        def rows_stats(d, carry):
            rows = pl.ds(pl.multiple_of(d * PIECE, PIECE), PIECE)
            if q == 0:
                values = feats[rows, :].astype(F32)
                first = jnp.sum(values, axis=1, keepdims=True)
                second = jnp.sum(values * values, axis=1, keepdims=True)
                mus[q, rows, :] = first / width
                flat = jnp.where(lane == 0, first, jnp.where(lane == 1, second, 0.0)).T
                first, second = flat[0:1, :], flat[1:2, :]
            else:
                values = feats[:, rows].astype(F32)
                first = jnp.sum(values, axis=0, keepdims=True)
                second = jnp.sum(values * values, axis=0, keepdims=True)
                flat = jnp.broadcast_to(first / width, (PIECE, PIECE)).T
                mus[q, rows, :] = flat[:, 0:1]
            misc_send[q, d, :, EMB : EMB + 128] = first
            misc_send[q, d, :, EMB + 128 : EMB + 256] = second
            return carry

        lax.fori_loop(0, 4, rows_stats, 0)
        contract = (((1,), (0,)), ((), ())) if q == 0 else (((0,), (0,)), ((), ()))

        def columns_step(n, carry):
            cols = pl.ds(pl.multiple_of(n * 256, 256), 256)
            block = weights[:, cols]
            total = jnp.dot(jnp.ones((8, width), BF16), block, preferred_element_type=F32)[0:1, :]
            part = lax.dot_general(feats[...], block, contract, preferred_element_type=F32) - mus[q] * total
            pf[q, :, cols] = part
            pb[q, :, cols] = part.astype(BF16)
            for d in range(4):
                misc_send[q, d, :, cols] = total
            return carry

        lax.fori_loop(0, 4, columns_step, 0)

    right, left, opposite = wrap(x + 1, 4), wrap(x + 3, 4), wrap(x + 2, 4)

    def part_rows(owner, start, count):
        return pl.ds(pl.multiple_of(owner * PIECE + start, 16), count)

    def scatter_misc(q):
        return [send(misc_send.at[q, wrap(x + d, 4)], misc_recv.at[q, x], (d, 0, 0, 0)) for d in (1, 3, 2)]

    def scatter_first(q, start, count, cut):
        low, high = pl.ds(start, cut), pl.ds(start + cut, count - cut)
        return {
            "batch": (q, start, count, cut),
            "relay0": send(pb.at[q, part_rows(opposite, start, cut), :], relay.at[q, 0, low, :], (1, 0, 0, 0)),
            "relay1": send(
                pb.at[q, part_rows(opposite, start + cut, count - cut), :], relay.at[q, 1, high, :], (3, 0, 0, 0)
            ),
            "fin0b": send(
                pb.at[q, part_rows(right, start + cut, count - cut), :], fin.at[q, 0, high, :], (1, 0, 0, 0)
            ),
            "fin1a": send(pb.at[q, part_rows(left, start, cut), :], fin.at[q, 1, low, :], (3, 0, 0, 0)),
        }

    def scatter_second(keys):
        q, start, count, cut = keys["batch"]
        low, high = pl.ds(start, cut), pl.ds(start + cut, count - cut)
        arrive(keys["relay0"], relay.at[q, 0, low, :])
        comb[q, low, :] = (pf[q, part_rows(right, start, cut), :] + relay[q, 0, low, :].astype(F32)).astype(BF16)
        keys["fin0a"] = send(comb.at[q, low, :], fin.at[q, 0, low, :], (1, 0, 0, 0))
        arrive(keys["relay1"], relay.at[q, 1, high, :])
        comb[q, high, :] = (
            pf[q, part_rows(left, start + cut, count - cut), :] + relay[q, 1, high, :].astype(F32)
        ).astype(BF16)
        keys["fin1b"] = send(comb.at[q, high, :], fin.at[q, 1, high, :], (3, 0, 0, 0))

    def settle(q, keys):
        for d, k in zip((1, 3, 2), keys):
            arrive(k, misc_recv.at[q, wrap(x - d, 4)])
        misc_recv[q, x] = misc_send[q, x]
        turn[...] = jnp.zeros_like(turn)
        first = [misc_recv[q, s, :, EMB : EMB + 128] for s in range(4)]
        second = [misc_recv[q, s, :, EMB + 128 : EMB + 256] for s in range(4)]
        mean = (first[0] + first[1] + first[2] + first[3]) / WIDTH[q]
        square = (second[0] + second[1] + second[2] + second[3]) / WIDTH[q]
        turn[4:5, :] = lax.rsqrt(square - mean * mean + 1e-06)
        for s in range(4):
            turn[s : s + 1, :] = first[s] / LOCAL[q] - mean
        columns[q] = turn[...].T

    def finish(keys):
        q, start, count, cut = keys["batch"]
        low, high, rows = pl.ds(start, cut), pl.ds(start + cut, count - cut), pl.ds(start, count)
        arrive(keys["fin0b"], fin.at[q, 0, high, :])
        arrive(keys["fin1a"], fin.at[q, 1, low, :])
        arrive(keys["fin0a"], fin.at[q, 0, low, :])
        arrive(keys["fin1b"], fin.at[q, 1, high, :])
        total = pf[q, part_rows(x, start, count), :] + fin[q, 0, rows, :].astype(F32) + fin[q, 1, rows, :].astype(F32)
        for s in range(4):
            total = total + columns[q, rows, s : s + 1] * misc_recv[q, s, :, 0:EMB]
        projected = total * columns[q, rows, 4:5]
        length = lax.rsqrt(jnp.sum(projected * projected, axis=1, keepdims=True) + 1e-06)
        return (projected * length).astype(BF16)

    def unit_a(dx, dy):
        return img_a, NA, wrap(y + dy, 4), wrap(x + dx, 4)

    def unit_b(dx, dy):
        return img_b, NB, wrap(x + dx, 4), wrap(y + dy, 4)

    CUT = {NA: CUT_A, NB: CUT_B}

    def chunk(where, part=None):
        ref, size, unit, place = where
        start, count = {None: (0, size), 0: (0, CUT[size]), 1: (CUT[size], size - CUT[size])}[part]
        return ref.at[unit, pl.ds(pl.multiple_of(place * size + start, 16), count), :]

    move = {"x": lambda s: (s, 0, 0, 0), "y": lambda s: (0, s, 0, 0)}

    def spread(axis, where):
        ref = chunk(where)
        return [send(ref, ref, move[axis](1)), send(ref, ref, move[axis](3))]

    def pass_on(axis, keys, lower, upper):
        arrive(keys[0], chunk(lower))
        low = send(chunk(lower, 0), chunk(lower, 0), move[axis](1))
        arrive(keys[1], chunk(upper))
        high = send(chunk(upper, 1), chunk(upper, 1), move[axis](3))
        return low, high

    def land(keys, far):
        arrive(keys[0], chunk(far, 0))
        arrive(keys[1], chunk(far, 1))

    def store_image(where, rows):
        ref, size, unit, place = where
        ref[unit, pl.ds(pl.multiple_of(place * size, 16), size), :] = rows

    def cap(dz, half, other=0, start=0, count=HALF):
        place = lax.rem(core + other, 2) * PIECE + half * HALF
        return txt.at[wrap(z + dz, 8), pl.ds(pl.multiple_of(place + start, 16), count), :]

    up, down, pair_keys = {}, {}, {}

    def captions_start(half, rows):
        txt[z, pl.ds(pl.multiple_of(core * PIECE + half * HALF, HALF), HALF), :] = rows
        up[half, 1] = send(cap(0, half), cap(0, half), (0, 0, 1, 0))
        down[half, 1] = send(cap(0, half), cap(0, half), (0, 0, 7, 0))
        pair_keys[half, 0] = send(cap(0, half), cap(0, half), (0, 0, 0, 1))

    def captions_step(half, d):
        if d < 4:
            arrive(up[half, d], cap(-d, half))
            if d < 3:
                up[half, d + 1] = send(cap(-d, half), cap(-d, half), (0, 0, 1, 0))
            else:
                up[half, 4] = send(cap(-3, half, 0, 0, QUART), cap(-3, half, 0, 0, QUART), (0, 0, 1, 0))
            arrive(down[half, d], cap(d, half))
            if d < 3:
                down[half, d + 1] = send(cap(d, half), cap(d, half), (0, 0, 7, 0))
            else:
                down[half, 4] = send(cap(3, half, 0, QUART, QUART), cap(3, half, 0, QUART, QUART), (0, 0, 7, 0))
            pair_keys[half, -d] = send(cap(-d, half), cap(-d, half), (0, 0, 0, 1))
            pair_keys[half, d] = send(cap(d, half), cap(d, half), (0, 0, 0, 1))
        else:
            arrive(up[half, 4], cap(4, half, 0, 0, QUART))
            arrive(down[half, 4], cap(4, half, 0, QUART, QUART))
            pair_keys[half, 4] = send(cap(4, half), cap(4, half), (0, 0, 0, 1))

    def sibling(*offsets):
        for dz in offsets:
            for half in (0, 1):
                arrive(pair_keys[half, dz], cap(dz, half, 1))

    scale = scale_ref[0, 0]
    scale2 = scale * LOG2E

    def signed(k):
        if isinstance(k, int):
            return ((k + 1) // 2) * (1 - 2 * ((k + 1) % 2))
        return ((k + 1) // 2) * (1 - 2 * lax.rem(k + 1, 2))

    def update(max_ref, sum_ref, unit, top, total):
        old, held = max_ref[unit], sum_ref[unit]
        gap = old - top
        small = jnp.exp2(-jnp.abs(gap))
        keep = gap >= 0
        max_ref[unit] = jnp.maximum(old, top)
        sum_ref[unit] = jnp.where(keep, held, total) + jnp.where(keep, total, held) * small

    def group(images, max_ref, sum_ref, unit, ks):
        units = [wrap(z + signed(k), 8) for k in ks]
        scores = [
            scale2 * lax.dot_general(images[unit], txt[v], (((1,), (1,)), ((), ())), preferred_element_type=F32)
            for v in units
        ]
        for v, block in zip(units, scores):
            top = jnp.max(block, axis=0, keepdims=True)
            update(cmax, csum, v, top, jnp.sum(jnp.exp2(block - top), axis=0, keepdims=True))
        widest = scores[0]
        for block in scores[1:]:
            widest = jnp.maximum(widest, block)
        top = jnp.max(widest, axis=1, keepdims=True)
        total = jnp.exp2(scores[0] - top)
        for block in scores[1:]:
            total = total + jnp.exp2(block - top)
        update(max_ref, sum_ref, unit, top, jnp.sum(total, axis=1, keepdims=True))

    def wave(j0, j1, *ks):
        def step(j, carry):
            group(img_a, rmax_a, rsum_a, wrap(y + signed(j), 4), ks)
            group(img_b, rmax_b, rsum_b, wrap(x + signed(j), 4), ks)
            return carry

        lax.fori_loop(j0, j1, step, 0)

    loads[0].wait()
    loads[1].wait()
    project(0, xi, wi)
    pl.semaphore_wait(barrier, len(plane) + len(column))
    first_a = scatter_first(0, 0, NA, CUT_A)
    misc_image = scatter_misc(0)
    loads[2].wait()
    loads[3].wait()
    project(1, xt, wt)
    first_t0 = scatter_first(1, 0, HALF, QUART)
    misc_text = scatter_misc(1)
    for ref in (rmax_a, rmax_b, cmax):
        ref[...] = jnp.full(ref.shape, LOW, F32)
    for ref in (rsum_a, rsum_b, csum):
        ref[...] = jnp.zeros(ref.shape, F32)
    scatter_second(first_a)
    settle(0, misc_image)
    first_b = scatter_first(0, NA, NB, CUT_B)
    scatter_second(first_t0)
    settle(1, misc_text)
    store_image(unit_a(0, 0), finish(first_a))
    a_x = spread("x", unit_a(0, 0))
    a_y = {0: spread("y", unit_a(0, 0))}
    a_far, b_far = {}, {}
    scatter_second(first_b)
    captions_start(0, finish(first_t0))
    first_t1 = scatter_first(1, HALF, HALF, QUART)
    store_image(unit_b(0, 0), finish(first_b))
    b_y = spread("y", unit_b(0, 0))
    b_x = {0: spread("x", unit_b(0, 0))}
    a_x_far = pass_on("x", a_x, unit_a(-1, 0), unit_a(1, 0))
    for s in (-1, 1):
        a_y[s] = spread("y", unit_a(s, 0))
    scatter_second(first_t1)
    captions_step(0, 1)
    a_far[0] = pass_on("y", a_y[0], unit_a(0, -1), unit_a(0, 1))
    b_y_far = pass_on("y", b_y, unit_b(0, -1), unit_b(0, 1))
    for s in (-1, 1):
        b_x[s] = spread("x", unit_b(0, s))
    land(a_x_far, unit_a(2, 0))
    a_y[2] = spread("y", unit_a(2, 0))
    captions_start(1, finish(first_t1))
    land(b_y_far, unit_b(0, 2))
    b_x[2] = spread("x", unit_b(0, 2))
    b_far[0] = pass_on("x", b_x[0], unit_b(-1, 0), unit_b(1, 0))
    captions_step(0, 2)
    sibling(0)
    wave(0, 1, 0)
    captions_step(1, 1)
    for s in (-1, 1):
        a_far[s] = pass_on("y", a_y[s], unit_a(s, -1), unit_a(s, 1))
        b_far[s] = pass_on("x", b_x[s], unit_b(-1, s), unit_b(1, s))
    captions_step(0, 3)
    sibling(-1, 1)
    wave(0, 1, 1, 2)
    captions_step(1, 2)
    a_far[2] = pass_on("y", a_y[2], unit_a(2, -1), unit_a(2, 1))
    b_far[2] = pass_on("x", b_x[2], unit_b(-1, 2), unit_b(1, 2))
    captions_step(0, 4)
    wave(1, 2, 0, 1, 2)
    captions_step(1, 3)
    wave(2, 3, 0, 1, 2)
    sibling(-2, 2)
    wave(0, 3, 3, 4)
    captions_step(1, 4)
    for s in (0, -1, 1):
        land(a_far[s], unit_a(s, 2))
        land(b_far[s], unit_b(2, s))

    own_caps = txt[z, pl.ds(pl.multiple_of(core * PIECE, PIECE), PIECE), :]
    turn[...] = jnp.zeros_like(turn)
    turn[0:8, :] = pairs_ref[...].astype(F32)
    partner = turn[...].T
    mine = (piece * PIECE + lane).astype(F32)
    caption_positive = jnp.zeros((1, PIECE), F32)
    image_positive = jnp.zeros((PIECE, PIECE), F32)
    for p in range(8):
        t, px = p // 4, p % 4
        rows = jnp.concatenate(
            [
                img_a[yh * 2 + t, px * NA : (px + 1) * NA, :],
                img_b[px, pl.ds(pl.multiple_of((yh * 2 + t) * NB, 16), NB), :],
            ],
            axis=0,
        )
        scores = scale * lax.dot_general(
            rows, own_caps, (((1,), (1,)), ((), ())), preferred_element_type=F32
        )
        picked = jnp.where(partner[:, p : p + 1] == mine, scores, 0.0)
        caption_positive = caption_positive + jnp.sum(picked, axis=0, keepdims=True)
        image_positive = jnp.where(lane == p, jnp.sum(picked, axis=1, keepdims=True), image_positive)
    image_positive = image_positive.T

    sibling(-3, 3, 4)
    wave(0, 3, 5, 6, 7)
    land(a_far[2], unit_a(2, 2))
    land(b_far[2], unit_b(2, 2))
    wave(3, 4, 0, 1, 2, 3, 4, 5, 6, 7)

    for u in range(8):
        logs = (cmax[u] + jnp.log2(csum[u])) * LN2
        csend[2 * u] = logs[:, 0:PIECE]
        csend[2 * u + 1] = logs[:, PIECE : 2 * PIECE]
    me_column = z * 2 + core
    column_keys = []
    for where in column:
        target = wrap(z + where[2], 8) * 2 + lax.rem(core + where[3], 2)
        column_keys.append(send(csend.at[target], crecv.at[me_column], where))

    def flat_logs(max_ref, sum_ref, size):
        wide = lax.broadcasted_iota(jnp.int32, (size, PIECE), 1)
        logs = jnp.zeros((size, PIECE), F32)
        for u in range(4):
            logs = jnp.where(wide == u, (max_ref[u] + jnp.log2(sum_ref[u])) * LN2, logs)
        padded = -(-size // PIECE) * PIECE
        if padded > size:
            logs = jnp.concatenate([logs, jnp.zeros((padded - size, PIECE), F32)], axis=0)
        return jnp.concatenate([logs[i : i + PIECE].T for i in range(0, padded, PIECE)], axis=1)

    flat_a = flat_logs(rmax_a, rsum_a, 4 * NA)
    flat_b = flat_logs(rmax_b, rsum_b, 4 * NB)
    same = [(yh == 0).astype(F32), (yh == 1).astype(F32)]
    for py in range(4):
        for px in range(4):
            rsend[py * 4 + px, 0:1, :] = jnp.concatenate(
                [flat_a[py : py + 1, px * NA : (px + 1) * NA], flat_b[px : px + 1, py * NB : (py + 1) * NB]], axis=1
            )
            p = (py % 2) * 4 + px
            rsend[py * 4 + px, 1:2, :] = image_positive[p : p + 1, :] * same[py // 2]
    me_plane = y * 4 + x
    plane_keys = []
    for where in plane:
        target = wrap(y + where[1], 4) * 4 + wrap(x + where[0], 4)
        plane_keys.append(send(rsend.at[target], rrecv.at[me_plane], where))
    crecv[me_column] = csend[me_column]
    rrecv[me_plane] = rsend[me_plane]
    for where, k in zip(column, column_keys):
        source = wrap(z - where[2], 8) * 2 + lax.rem(core + where[3], 2)
        arrive(k, crecv.at[source])
    for where, k in zip(plane, plane_keys):
        source = wrap(y - where[1], 4) * 4 + wrap(x - where[0], 4)
        arrive(k, rrecv.at[source])

    def merge(rows):
        top = jnp.max(rows, axis=0)
        return top + jnp.log(jnp.sum(jnp.exp(rows - top[None]), axis=0))

    image_rows = rrecv[...]
    fsend[0:1, :] = merge(image_rows[:, 0:1, :]) - jnp.sum(image_rows[:, 1:2, :], axis=0)
    fsend[1:2, :] = merge(crecv[...]) - caption_positive
    shard = [(dx, dt) for dt in range(2) for dx in range(4) if (dx, dt) != (0, 0)]
    shard_keys = []
    step_y = [0, 1 - 2 * tw]
    for dx, dt in shard:
        shard_keys.append(send(fsend, frecv.at[piece], (dx, step_y[dt], 0, 0)))
    frecv[piece] = fsend[...]
    for (dx, dt), k in zip(shard, shard_keys):
        source = lax.rem(tw + dt, 2) * 4 + wrap(x - dx, 4)
        arrive(k, frecv.at[source])
    for p in range(8):
        out[p : p + 1, :] = frecv[p, 0:1, :]
        out[8 + p : 9 + p, :] = frecv[p, 1:2, :]
    for copy in sent:
        copy.wait_send()


def on_device(image_feats, text_feats, image_proj, text_proj, logit_scale, pairs):
    vmem = pl.BlockSpec(memory_space=pltpu.VMEM)
    hbm = pl.BlockSpec(memory_space=pl.ANY)
    losses = pl.pallas_call(
        kernel,
        out_shape=jax.ShapeDtypeStruct((16, 128), F32),
        in_specs=[hbm, hbm, hbm, hbm, pl.BlockSpec(memory_space=pltpu.SMEM), vmem],
        out_specs=vmem,
        scratch_shapes=[
            pltpu.VMEM((512, LOCAL[0]), BF16),
            pltpu.VMEM((LOCAL[1], 512), BF16),
            pltpu.VMEM((LOCAL[0], EMB), BF16),
            pltpu.VMEM((LOCAL[1], EMB), BF16),
            pltpu.VMEM((2, 512, 1), F32),
            pltpu.VMEM((2, 512, EMB), F32),
            pltpu.VMEM((2, 512, EMB), BF16),
            pltpu.VMEM((2, 4, 1, EMB + 256), F32),
            pltpu.VMEM((2, 4, 1, EMB + 256), F32),
            pltpu.VMEM((2, 2, PIECE, EMB), BF16),
            pltpu.VMEM((2, PIECE, EMB), BF16),
            pltpu.VMEM((2, 2, PIECE, EMB), BF16),
            pltpu.VMEM((PIECE, PIECE), F32),
            pltpu.VMEM((2, PIECE, PIECE), F32),
            pltpu.VMEM((4, 4 * NA, EMB), BF16),
            pltpu.VMEM((4, 4 * NB, EMB), BF16),
            pltpu.VMEM((8, 256, EMB), BF16),
            pltpu.VMEM((4, 4 * NA, 1), F32),
            pltpu.VMEM((4, 4 * NA, 1), F32),
            pltpu.VMEM((4, 4 * NB, 1), F32),
            pltpu.VMEM((4, 4 * NB, 1), F32),
            pltpu.VMEM((8, 1, 256), F32),
            pltpu.VMEM((8, 1, 256), F32),
            pltpu.VMEM((16, 2, PIECE), F32),
            pltpu.VMEM((16, 2, PIECE), F32),
            pltpu.VMEM((16, 1, PIECE), F32),
            pltpu.VMEM((16, 1, PIECE), F32),
            pltpu.VMEM((2, PIECE), F32),
            pltpu.VMEM((8, 2, PIECE), F32),
            pltpu.SemaphoreType.DMA((4,)),
            pltpu.SemaphoreType.DMA((NSEM,)),
            pltpu.SemaphoreType.DMA((NSEM,)),
        ],
        compiler_params=pltpu.CompilerParams(
            collective_id=0, has_side_effects=True, vmem_limit_bytes=60 * 1024 * 1024
        ),
    )(
        image_feats, text_feats.T, image_proj, text_proj,
        logit_scale.reshape(1, 1), pairs.reshape(8, 128),
    )
    return (losses[0:8].reshape(ROWS), losses[8:16].reshape(ROWS))


def solution(mesh):
    return jax.shard_map(
        on_device,
        mesh=mesh,
        in_specs=(
            P("blk", "mp"),
            P("blk", "mp"),
            P("mp", None),
            P("mp", None),
            P(),
            P("blk", None),
        ),
        out_specs=(P("blk"), P("blk")),
        check_vma=False,
    )
```

```python
import jax
import jax.numpy as jnp
from jax import lax
from jax.experimental import pallas as pl
from jax.experimental.pallas import tpu as pltpu
from jax.sharding import PartitionSpec as P

MESH = pl.DeviceIdType.MESH
F32 = jnp.float32
BF16 = jnp.bfloat16
ROWS = 1024
EMB = 1024
WIDTH = (5120, 1280)
LOCAL = (1280, 320)
PIECE = 128
HALF = 64
QUART = 32
NSEM = 160
NA, NB = 64, 64
CUT_A, CUT_B = 32, 32
IMAGE_A, IMAGE_B, TEXT_0, TEXT_1 = range(4)
KIND_A, KIND_B = 0, 1
(
    FIRST, FROM_LEFT, FROM_RIGHT, FINISH, STAGE_LOW, STAGE_HIGH, STAGE_FAR, PASS_LOW, PASS_HIGH, LAND,
    CAPTION_LOW, CAPTION_HIGH, CAPTION_FAR, SIBLING, TILE, POSITIVE,
) = range(16)
ORDER = [
    (FIRST, IMAGE_A),
    (FIRST, TEXT_0),
    (FIRST, IMAGE_B),
    (FIRST, TEXT_1),
    (FROM_RIGHT, IMAGE_A),
    (FROM_LEFT, IMAGE_A),
    (FROM_RIGHT, TEXT_0),
    (FROM_LEFT, TEXT_0),
    (FROM_LEFT, IMAGE_B),
    (FROM_RIGHT, IMAGE_B),
    (FROM_RIGHT, TEXT_1),
    (FROM_LEFT, TEXT_1),
    (FINISH, IMAGE_A),
    (FINISH, TEXT_0),
    (FINISH, IMAGE_B),
    (SIBLING, 0, 0),
    (FINISH, TEXT_1),
    (SIBLING, 1, 0),
    (PASS_LOW, KIND_A, 0),
    (STAGE_LOW, KIND_A),
    (CAPTION_LOW, 0, 1),
    (STAGE_HIGH, KIND_A),
    (CAPTION_HIGH, 0, 1),
    (SIBLING, 0, 1),
    (STAGE_LOW, KIND_B),
    (STAGE_HIGH, KIND_B),
    (CAPTION_HIGH, 1, 1),
    (PASS_LOW, KIND_B, 0),
    (CAPTION_LOW, 1, 1),
    (STAGE_FAR, KIND_A),
    (TILE, KIND_A, 0, (0,)),
    (CAPTION_LOW, 0, 2),
    (CAPTION_HIGH, 0, 2),
    (SIBLING, 0, -2),
    (PASS_LOW, KIND_B, -1),
    (PASS_HIGH, KIND_B, -1),
    (SIBLING, 1, -1),
    (SIBLING, 1, 1),
    (SIBLING, 0, -1),
    (PASS_HIGH, KIND_A, 0),
    (PASS_HIGH, KIND_B, 0),
    (SIBLING, 0, 2),
    (TILE, KIND_A, 0, (-1, 1)),
    (PASS_HIGH, KIND_A, 1),
    (CAPTION_LOW, 1, 2),
    (CAPTION_HIGH, 1, 2),
    (PASS_LOW, KIND_A, 1),
    (STAGE_FAR, KIND_B),
    (PASS_LOW, KIND_B, 1),
    (SIBLING, 1, 2),
    (PASS_HIGH, KIND_A, -1),
    (SIBLING, 1, -2),
    (PASS_LOW, KIND_A, -1),
    (PASS_HIGH, KIND_B, 1),
    (TILE, KIND_B, 0, (0, -1, 1, -2)),
    (TILE, KIND_A, 0, (-2, 2)),
    (CAPTION_HIGH, 0, 3),
    (TILE, KIND_B, 0, (2,)),
    (PASS_HIGH, KIND_A, 2),
    (CAPTION_LOW, 0, 3),
    (TILE, KIND_A, 1, (0, -1, 1, -2)),
    (PASS_LOW, KIND_A, 2),
    (TILE, KIND_A, -1, (0, -1, 1, -2)),
    (TILE, KIND_A, -1, (2,)),
    (TILE, KIND_A, 1, (2,)),
    (LAND, KIND_A, 1),
    (CAPTION_LOW, 1, 3),
    (LAND, KIND_B, -1),
    (CAPTION_HIGH, 1, 3),
    (PASS_LOW, KIND_B, 2),
    (LAND, KIND_A, 0),
    (PASS_HIGH, KIND_B, 2),
    (TILE, KIND_B, -1, (0, -1, 1, -2)),
    (CAPTION_FAR, 0),
    (SIBLING, 1, -3),
    (SIBLING, 0, -3),
    (SIBLING, 1, 3),
    (TILE, KIND_B, 1, (0, -1, 1, -2)),
    (TILE, KIND_B, -1, (2, -3)),
    (LAND, KIND_A, 2),
    (LAND, KIND_B, 1),
    (LAND, KIND_A, -1),
    (SIBLING, 0, 3),
    (LAND, KIND_B, 0),
    (POSITIVE,),
    (TILE, KIND_A, 2, (0, -1, 1, -2)),
    (LAND, KIND_B, 2),
    (SIBLING, 0, 4),
    (CAPTION_FAR, 1),
    (TILE, KIND_B, 2, (0, -1, 1, -2)),
    (SIBLING, 1, 4),
    (TILE, KIND_A, 2, (2, -3, 3, 4)),
    (TILE, KIND_B, 1, (2, -3, 3, 4)),
    (TILE, KIND_B, 2, (2, -3, 3, 4)),
    (TILE, KIND_A, 0, (-3, 3, 4)),
    (TILE, KIND_A, -1, (-3, 3, 4)),
    (TILE, KIND_A, 1, (-3, 3, 4)),
    (TILE, KIND_B, 0, (-3, 3, 4)),
    (TILE, KIND_B, -1, (3, 4)),
]
LOG2E = 1.4426950408889634
LN2 = 0.6931471805599453
LOW = -1e30


def wrap(value, count):
    return lax.rem(value + count, count)


def kernel(
    imf, txf, wim, wtx, scale_ref, pairs_ref, out,
    xi, xt, xtt, wi, wt, mus, pf, pb, misc_send, misc_recv, relay, comb, fin, turn, columns,
    img_a, img_b, txt, rmax_a, rsum_a, rmax_b, rsum_b, cmax, csum,
    rsend, rrecv, csend, crecv, fsend, frecv, lsem, ssem, rsem,
):
    tw = lax.axis_index("tower")
    blk = lax.axis_index("blk")
    x = lax.axis_index("mp")
    core = lax.rem(blk, 2)
    yh = lax.rem(blk // 2, 2)
    z = blk // 4
    y = yh * 2 + tw
    piece = tw * 4 + x

    def device(dx, dy, dz, dc):
        px = wrap(x + dx, 4)
        py = wrap(y + dy, 4)
        pz = wrap(z + dz, 8)
        pc = lax.rem(core + dc, 2)
        return {"tower": lax.rem(py, 2), "blk": (pz * 2 + py // 2) * 2 + pc, "mp": px}

    sent = []

    def send(src, dst, where):
        k = len(sent)
        copy = pltpu.make_async_remote_copy(
            src_ref=src, dst_ref=dst, send_sem=ssem.at[k], recv_sem=rsem.at[k],
            device_id=device(*where), device_id_type=MESH,
        )
        copy.start()
        sent.append(copy)
        return k

    def arrive(k, ref):
        pltpu.make_async_remote_copy(
            src_ref=ref, dst_ref=ref, send_sem=ssem.at[k], recv_sem=rsem.at[k],
            device_id=device(1, 0, 0, 0), device_id_type=MESH,
        ).wait_recv()

    half_rows = pl.ds(pl.multiple_of(tw * 512, 512), 512)
    loads = [
        pltpu.make_async_copy(imf.at[half_rows, :], xi, lsem.at[0]),
        pltpu.make_async_copy(wim, wi, lsem.at[1]),
        pltpu.make_async_copy(txf.at[:, half_rows], xt, lsem.at[2]),
        pltpu.make_async_copy(wtx, wt, lsem.at[3]),
    ]
    for load in loads:
        load.start()

    plane = [(dx, dy, 0, 0) for dy in range(4) for dx in range(4) if (dx, dy) != (0, 0)]
    column = [(0, 0, dz, dc) for dz in range(8) for dc in range(2) if (dz, dc) != (0, 0)]
    barrier = pltpu.get_barrier_semaphore()
    for to in plane + column:
        pl.semaphore_signal(barrier, inc=1, device_id=device(*to), device_id_type=MESH)

    lane = lax.broadcasted_iota(jnp.int32, (PIECE, PIECE), 1)

    def project(q, feats, weights):
        width = LOCAL[q]

        def rows_stats(d, carry):
            rows = pl.ds(pl.multiple_of(d * PIECE, PIECE), PIECE)
            if q == 0:
                values = feats[rows, :].astype(F32)
                first = jnp.sum(values, axis=1, keepdims=True)
                second = jnp.sum(values * values, axis=1, keepdims=True)
                mus[q, rows, :] = first / width
                flat = jnp.where(lane == 0, first, jnp.where(lane == 1, second, 0.0)).T
                first, second = flat[0:1, :], flat[1:2, :]
            else:
                values = feats[:, rows].astype(F32)
                first = jnp.sum(values, axis=0, keepdims=True)
                second = jnp.sum(values * values, axis=0, keepdims=True)
                flat = jnp.broadcast_to(first / width, (PIECE, PIECE)).T
                mus[q, rows, :] = flat[:, 0:1]
            misc_send[q, d, :, EMB : EMB + 128] = first
            misc_send[q, d, :, EMB + 128 : EMB + 256] = second
            return carry

        lax.fori_loop(0, 4, rows_stats, 0)
        lhs = feats
        if q == 1:
            lhs = xtt
            lhs[...] = feats[...].T

        def columns_step(n, carry):
            cols = pl.ds(pl.multiple_of(n * 256, 256), 256)
            block = weights[:, cols]
            total = jnp.dot(jnp.ones((8, width), BF16), block, preferred_element_type=F32)[0:1, :]
            part = jnp.dot(lhs[...], block, preferred_element_type=F32) - mus[q] * total
            pf[q, :, cols] = part
            pb[q, :, cols] = part.astype(BF16)
            for d in range(4):
                misc_send[q, d, :, cols] = total
            return carry

        lax.fori_loop(0, 4, columns_step, 0)

    right, left, opposite = wrap(x + 1, 4), wrap(x + 3, 4), wrap(x + 2, 4)

    def part_rows(owner, start, count):
        return pl.ds(pl.multiple_of(owner * PIECE + start, 16), count)

    def scatter_misc(q):
        return [send(misc_send.at[q, wrap(x + d, 4)], misc_recv.at[q, x], (d, 0, 0, 0)) for d in (1, 3, 2)]

    def scatter_first(q, start, count, cut):
        low, high = pl.ds(start, cut), pl.ds(start + cut, count - cut)
        return {
            "batch": (q, start, count, cut),
            "relay0": send(pb.at[q, part_rows(opposite, start, cut), :], relay.at[q, 0, low, :], (1, 0, 0, 0)),
            "relay1": send(
                pb.at[q, part_rows(opposite, start + cut, count - cut), :], relay.at[q, 1, high, :], (3, 0, 0, 0)
            ),
            "fin0b": send(
                pb.at[q, part_rows(right, start + cut, count - cut), :], fin.at[q, 0, high, :], (1, 0, 0, 0)
            ),
            "fin1a": send(pb.at[q, part_rows(left, start, cut), :], fin.at[q, 1, low, :], (3, 0, 0, 0)),
        }

    def settle(q, keys):
        for d, k in zip((1, 3, 2), keys):
            arrive(k, misc_recv.at[q, wrap(x - d, 4)])
        misc_recv[q, x] = misc_send[q, x]
        turn[...] = jnp.zeros_like(turn)
        first = [misc_recv[q, s, :, EMB : EMB + 128] for s in range(4)]
        second = [misc_recv[q, s, :, EMB + 128 : EMB + 256] for s in range(4)]
        mean = (first[0] + first[1] + first[2] + first[3]) / WIDTH[q]
        square = (second[0] + second[1] + second[2] + second[3]) / WIDTH[q]
        turn[4:5, :] = lax.rsqrt(square - mean * mean + 1e-06)
        for s in range(4):
            turn[s : s + 1, :] = first[s] / LOCAL[q] - mean
        columns[q] = turn[...].T

    def finish(keys):
        q, start, count, cut = keys["batch"]
        low, high, rows = pl.ds(start, cut), pl.ds(start + cut, count - cut), pl.ds(start, count)
        arrive(keys["fin0b"], fin.at[q, 0, high, :])
        arrive(keys["fin1a"], fin.at[q, 1, low, :])
        arrive(keys["fin0a"], fin.at[q, 0, low, :])
        arrive(keys["fin1b"], fin.at[q, 1, high, :])
        total = pf[q, part_rows(x, start, count), :] + fin[q, 0, rows, :].astype(F32) + fin[q, 1, rows, :].astype(F32)
        for s in range(4):
            total = total + columns[q, rows, s : s + 1] * misc_recv[q, s, :, 0:EMB]
        projected = total * columns[q, rows, 4:5]
        length = lax.rsqrt(jnp.sum(projected * projected, axis=1, keepdims=True) + 1e-06)
        return (projected * length).astype(BF16)

    def unit_a(dx, dy):
        return img_a, NA, wrap(y + dy, 4), wrap(x + dx, 4)

    def unit_b(dx, dy):
        return img_b, NB, wrap(x + dx, 4), wrap(y + dy, 4)

    CUT = {NA: CUT_A, NB: CUT_B}

    def chunk(where, part=None):
        ref, size, unit, place = where
        start, count = {None: (0, size), 0: (0, CUT[size]), 1: (CUT[size], size - CUT[size])}[part]
        return ref.at[unit, pl.ds(pl.multiple_of(place * size + start, 16), count), :]

    move = {"x": lambda s: (s, 0, 0, 0), "y": lambda s: (0, s, 0, 0)}

    def spread(axis, where):
        ref = chunk(where)
        return [send(ref, ref, move[axis](1)), send(ref, ref, move[axis](3))]

    def store_image(where, rows):
        ref, size, unit, place = where
        ref[unit, pl.ds(pl.multiple_of(place * size, 16), size), :] = rows

    def cap(dz, half, other=0, start=0, count=HALF):
        place = lax.rem(core + other, 2) * PIECE + half * HALF
        return txt.at[wrap(z + dz, 8), pl.ds(pl.multiple_of(place + start, 16), count), :]

    scale = scale_ref[0, 0]
    scale2 = scale * LOG2E

    def update(max_ref, sum_ref, unit, top, total):
        old, held = max_ref[unit], sum_ref[unit]
        gap = old - top
        small = jnp.exp2(-jnp.abs(gap))
        keep = gap >= 0
        max_ref[unit] = jnp.maximum(old, top)
        sum_ref[unit] = jnp.where(keep, held, total) + jnp.where(keep, total, held) * small

    def group(images, max_ref, sum_ref, unit, offsets):
        units = [wrap(z + dz, 8) for dz in offsets]
        scores = [
            scale2 * lax.dot_general(images[unit], txt[v], (((1,), (1,)), ((), ())), preferred_element_type=F32)
            for v in units
        ]
        for v, block in zip(units, scores):
            top = jnp.max(block, axis=0, keepdims=True)
            update(cmax, csum, v, top, jnp.sum(jnp.exp2(block - top), axis=0, keepdims=True))
        widest = scores[0]
        for block in scores[1:]:
            widest = jnp.maximum(widest, block)
        top = jnp.max(widest, axis=1, keepdims=True)
        total = jnp.exp2(scores[0] - top)
        for block in scores[1:]:
            total = total + jnp.exp2(block - top)
        update(max_ref, sum_ref, unit, top, jnp.sum(total, axis=1, keepdims=True))

    tasks = {}
    BATCH = {
        IMAGE_A: (0, 0, NA, CUT_A),
        IMAGE_B: (0, NA, NB, CUT_B),
        TEXT_0: (1, 0, HALF, QUART),
        TEXT_1: (1, HALF, HALF, QUART),
    }

    def start_batch(name):
        q, start, count, cut = BATCH[name]
        low, high = pl.ds(start, cut), pl.ds(start + cut, count - cut)
        keys = scatter_first(q, start, count, cut)

        def from_left():
            arrive(keys["relay0"], relay.at[q, 0, low, :])
            comb[q, low, :] = (
                pf[q, part_rows(right, start, cut), :] + relay[q, 0, low, :].astype(F32)
            ).astype(BF16)
            keys["fin0a"] = send(comb.at[q, low, :], fin.at[q, 0, low, :], (1, 0, 0, 0))

        def from_right():
            arrive(keys["relay1"], relay.at[q, 1, high, :])
            comb[q, high, :] = (
                pf[q, part_rows(left, start + cut, count - cut), :] + relay[q, 1, high, :].astype(F32)
            ).astype(BF16)
            keys["fin1b"] = send(comb.at[q, high, :], fin.at[q, 1, high, :], (3, 0, 0, 0))

        def last():
            if name in (IMAGE_A, TEXT_0):
                settle(q, misc_keys[q])
            rows = finish(keys)
            if name == IMAGE_A:
                store_image(unit_a(0, 0), rows)
                stage("x", KIND_A, spread("x", unit_a(0, 0)))
                second_stage("y", KIND_A, 0, spread("y", unit_a(0, 0)))
            elif name == IMAGE_B:
                store_image(unit_b(0, 0), rows)
                stage("y", KIND_B, spread("y", unit_b(0, 0)))
                second_stage("x", KIND_B, 0, spread("x", unit_b(0, 0)))
            else:
                half = name - TEXT_0
                txt[z, pl.ds(pl.multiple_of(core * PIECE + half * HALF, HALF), HALF), :] = rows
                ref = cap(0, half)
                low_key, high_key = send(ref, ref, (0, 0, 1, 0)), send(ref, ref, (0, 0, 7, 0))
                to_sibling(half, 0)
                captions(half, 1, low_key, high_key)

        tasks[FROM_LEFT, name] = from_left
        tasks[FROM_RIGHT, name] = from_right
        tasks[FINISH, name] = last

    def where(kind, along, across):
        return unit_a(along, across) if kind == KIND_A else unit_b(across, along)

    def stage(axis, kind, keys):
        other = "y" if axis == "x" else "x"
        far = {}

        def lower():
            ref = where(kind, -1, 0)
            arrive(keys[0], chunk(ref))
            far[0] = send(chunk(ref, 0), chunk(ref, 0), move[axis](1))
            second_stage(other, kind, -1, spread(other, ref))

        def upper():
            ref = where(kind, 1, 0)
            arrive(keys[1], chunk(ref))
            far[1] = send(chunk(ref, 1), chunk(ref, 1), move[axis](3))
            second_stage(other, kind, 1, spread(other, ref))

        def opposite_chunk():
            ref = where(kind, 2, 0)
            arrive(far[0], chunk(ref, 0))
            arrive(far[1], chunk(ref, 1))
            second_stage(other, kind, 2, spread(other, ref))

        tasks[STAGE_LOW, kind] = lower
        tasks[STAGE_HIGH, kind] = upper
        tasks[STAGE_FAR, kind] = opposite_chunk

    def second_stage(axis, kind, s, keys):
        far = {}

        def lower():
            ref = where(kind, s, -1)
            arrive(keys[0], chunk(ref))
            far[0] = send(chunk(ref, 0), chunk(ref, 0), move[axis](1))

        def upper():
            ref = where(kind, s, 1)
            arrive(keys[1], chunk(ref))
            far[1] = send(chunk(ref, 1), chunk(ref, 1), move[axis](3))

        def land():
            ref = where(kind, s, 2)
            arrive(far[0], chunk(ref, 0))
            arrive(far[1], chunk(ref, 1))

        tasks[PASS_LOW, kind, s] = lower
        tasks[PASS_HIGH, kind, s] = upper
        tasks[LAND, kind, s] = land

    def to_sibling(half, dz):
        key = send(cap(dz, half), cap(dz, half), (0, 0, 0, 1))
        tasks[SIBLING, half, dz] = lambda: arrive(key, cap(dz, half, 1))

    def captions(half, d, low_key, high_key):
        keys = {}

        def follow():
            if len(keys) < 2:
                return
            if d < 3:
                captions(half, d + 1, keys[0], keys[1])
                return

            def opposite_caption():
                arrive(keys[0], cap(4, half, 0, 0, QUART))
                arrive(keys[1], cap(4, half, 0, QUART, QUART))
                to_sibling(half, 4)

            tasks[CAPTION_FAR, half] = opposite_caption

        def lower():
            arrive(low_key, cap(-d, half))
            ref = cap(-d, half) if d < 3 else cap(-d, half, 0, 0, QUART)
            keys[0] = send(ref, ref, (0, 0, 1, 0))
            to_sibling(half, -d)
            follow()

        def upper():
            arrive(high_key, cap(d, half))
            ref = cap(d, half) if d < 3 else cap(d, half, 0, QUART, QUART)
            keys[1] = send(ref, ref, (0, 0, 7, 0))
            to_sibling(half, d)
            follow()

        tasks[CAPTION_LOW, half, d] = lower
        tasks[CAPTION_HIGH, half, d] = upper

    def positives():
        own_caps = txt[z, pl.ds(pl.multiple_of(core * PIECE, PIECE), PIECE), :]
        turn[...] = jnp.zeros_like(turn)
        turn[0:8, :] = pairs_ref[...].astype(F32)
        partner = turn[...].T
        mine = (piece * PIECE + lane).astype(F32)
        caption_positive = jnp.zeros((1, PIECE), F32)
        image_positive = jnp.zeros((PIECE, PIECE), F32)
        for p in range(8):
            t, px = p // 4, p % 4
            rows = jnp.concatenate(
                [
                    img_a[yh * 2 + t, px * NA : (px + 1) * NA, :],
                    img_b[px, pl.ds(pl.multiple_of((yh * 2 + t) * NB, 16), NB), :],
                ],
                axis=0,
            )
            scores = scale * lax.dot_general(
                rows, own_caps, (((1,), (1,)), ((), ())), preferred_element_type=F32
            )
            picked = jnp.where(partner[:, p : p + 1] == mine, scores, 0.0)
            caption_positive = caption_positive + jnp.sum(picked, axis=0, keepdims=True)
            image_positive = jnp.where(lane == p, jnp.sum(picked, axis=1, keepdims=True), image_positive)
        image_positive = image_positive.T

        return caption_positive, image_positive

    loads[0].wait()
    loads[1].wait()
    project(0, xi, wi)
    pl.semaphore_wait(barrier, len(plane) + len(column))
    misc_keys = {}
    for item in ORDER:
        if item[0] == TILE:
            _, kind, offset, offsets = item
            if kind == KIND_A:
                group(img_a, rmax_a, rsum_a, wrap(y + offset, 4), offsets)
            else:
                group(img_b, rmax_b, rsum_b, wrap(x + offset, 4), offsets)
        elif item[0] == POSITIVE:
            caption_positive, image_positive = positives()
        elif item[0] == FIRST:
            start_batch(item[1])
            if item[1] == IMAGE_A:
                misc_keys[0] = scatter_misc(0)
                loads[2].wait()
                loads[3].wait()
                project(1, xt, wt)
                misc_keys[1] = scatter_misc(1)
                for ref in (rmax_a, rmax_b, cmax):
                    ref[...] = jnp.full(ref.shape, LOW, F32)
                for ref in (rsum_a, rsum_b, csum):
                    ref[...] = jnp.zeros(ref.shape, F32)
        else:
            tasks.pop(item)()

    for u in range(8):
        logs = (cmax[u] + jnp.log2(csum[u])) * LN2
        csend[2 * u] = logs[:, 0:PIECE]
        csend[2 * u + 1] = logs[:, PIECE : 2 * PIECE]
    me_column = z * 2 + core
    column_keys = []
    for to in column:
        target = wrap(z + to[2], 8) * 2 + lax.rem(core + to[3], 2)
        column_keys.append(send(csend.at[target], crecv.at[me_column], to))

    def flat_logs(max_ref, sum_ref, size):
        wide = lax.broadcasted_iota(jnp.int32, (size, PIECE), 1)
        logs = jnp.zeros((size, PIECE), F32)
        for u in range(4):
            logs = jnp.where(wide == u, (max_ref[u] + jnp.log2(sum_ref[u])) * LN2, logs)
        padded = -(-size // PIECE) * PIECE
        if padded > size:
            logs = jnp.concatenate([logs, jnp.zeros((padded - size, PIECE), F32)], axis=0)
        return jnp.concatenate([logs[i : i + PIECE].T for i in range(0, padded, PIECE)], axis=1)

    flat_a = flat_logs(rmax_a, rsum_a, 4 * NA)
    flat_b = flat_logs(rmax_b, rsum_b, 4 * NB)
    same = [(yh == 0).astype(F32), (yh == 1).astype(F32)]
    for py in range(4):
        for px in range(4):
            rsend[py * 4 + px, 0:1, :] = jnp.concatenate(
                [flat_a[py : py + 1, px * NA : (px + 1) * NA], flat_b[px : px + 1, py * NB : (py + 1) * NB]], axis=1
            )
            p = (py % 2) * 4 + px
            rsend[py * 4 + px, 1:2, :] = image_positive[p : p + 1, :] * same[py // 2]
    me_plane = y * 4 + x
    plane_keys = []
    for to in plane:
        target = wrap(y + to[1], 4) * 4 + wrap(x + to[0], 4)
        plane_keys.append(send(rsend.at[target], rrecv.at[me_plane], to))
    crecv[me_column] = csend[me_column]
    rrecv[me_plane] = rsend[me_plane]
    for to, k in zip(column, column_keys):
        source = wrap(z - to[2], 8) * 2 + lax.rem(core + to[3], 2)
        arrive(k, crecv.at[source])
    for to, k in zip(plane, plane_keys):
        source = wrap(y - to[1], 4) * 4 + wrap(x - to[0], 4)
        arrive(k, rrecv.at[source])

    def merge(rows):
        top = jnp.max(rows, axis=0)
        return top + jnp.log(jnp.sum(jnp.exp(rows - top[None]), axis=0))

    image_rows = rrecv[...]
    fsend[0:1, :] = merge(image_rows[:, 0:1, :]) - jnp.sum(image_rows[:, 1:2, :], axis=0)
    fsend[1:2, :] = merge(crecv[...]) - caption_positive
    shard = [(dx, dt) for dt in range(2) for dx in range(4) if (dx, dt) != (0, 0)]
    shard_keys = []
    step_y = [0, 1 - 2 * tw]
    for dx, dt in shard:
        shard_keys.append(send(fsend, frecv.at[piece], (dx, step_y[dt], 0, 0)))
    frecv[piece] = fsend[...]
    for (dx, dt), k in zip(shard, shard_keys):
        source = lax.rem(tw + dt, 2) * 4 + wrap(x - dx, 4)
        arrive(k, frecv.at[source])
    for p in range(8):
        out[p : p + 1, :] = frecv[p, 0:1, :]
        out[8 + p : 9 + p, :] = frecv[p, 1:2, :]
    for copy in sent:
        copy.wait_send()


def on_device(image_feats, text_feats, image_proj, text_proj, logit_scale, pairs):
    vmem = pl.BlockSpec(memory_space=pltpu.VMEM)
    hbm = pl.BlockSpec(memory_space=pl.ANY)
    losses = pl.pallas_call(
        kernel,
        out_shape=jax.ShapeDtypeStruct((16, 128), F32),
        in_specs=[hbm, hbm, hbm, hbm, pl.BlockSpec(memory_space=pltpu.SMEM), vmem],
        out_specs=vmem,
        scratch_shapes=[
            pltpu.VMEM((512, LOCAL[0]), BF16),
            pltpu.VMEM((LOCAL[1], 512), BF16),
            pltpu.VMEM((512, LOCAL[1]), BF16),
            pltpu.VMEM((LOCAL[0], EMB), BF16),
            pltpu.VMEM((LOCAL[1], EMB), BF16),
            pltpu.VMEM((2, 512, 1), F32),
            pltpu.VMEM((2, 512, EMB), F32),
            pltpu.VMEM((2, 512, EMB), BF16),
            pltpu.VMEM((2, 4, 1, EMB + 256), F32),
            pltpu.VMEM((2, 4, 1, EMB + 256), F32),
            pltpu.VMEM((2, 2, PIECE, EMB), BF16),
            pltpu.VMEM((2, PIECE, EMB), BF16),
            pltpu.VMEM((2, 2, PIECE, EMB), BF16),
            pltpu.VMEM((PIECE, PIECE), F32),
            pltpu.VMEM((2, PIECE, PIECE), F32),
            pltpu.VMEM((4, 4 * NA, EMB), BF16),
            pltpu.VMEM((4, 4 * NB, EMB), BF16),
            pltpu.VMEM((8, 256, EMB), BF16),
            pltpu.VMEM((4, 4 * NA, 1), F32),
            pltpu.VMEM((4, 4 * NA, 1), F32),
            pltpu.VMEM((4, 4 * NB, 1), F32),
            pltpu.VMEM((4, 4 * NB, 1), F32),
            pltpu.VMEM((8, 1, 256), F32),
            pltpu.VMEM((8, 1, 256), F32),
            pltpu.VMEM((16, 2, PIECE), F32),
            pltpu.VMEM((16, 2, PIECE), F32),
            pltpu.VMEM((16, 1, PIECE), F32),
            pltpu.VMEM((16, 1, PIECE), F32),
            pltpu.VMEM((2, PIECE), F32),
            pltpu.VMEM((8, 2, PIECE), F32),
            pltpu.SemaphoreType.DMA((4,)),
            pltpu.SemaphoreType.DMA((NSEM,)),
            pltpu.SemaphoreType.DMA((NSEM,)),
        ],
        compiler_params=pltpu.CompilerParams(
            collective_id=0, has_side_effects=True, vmem_limit_bytes=60 * 1024 * 1024
        ),
    )(
        image_feats, text_feats.T, image_proj, text_proj,
        logit_scale.reshape(1, 1), pairs.reshape(8, 128),
    )
    return (losses[0:8].reshape(ROWS), losses[8:16].reshape(ROWS))


def solution(mesh):
    return jax.shard_map(
        on_device,
        mesh=mesh,
        in_specs=(
            P("blk", "mp"),
            P("blk", "mp"),
            P("mp", None),
            P("mp", None),
            P(),
            P("blk", None),
        ),
        out_specs=(P("blk"), P("blk")),
        check_vma=False,
    )
```

```python
import jax
import jax.numpy as jnp
from jax import lax
from jax.experimental import pallas as pl
from jax.experimental.pallas import tpu as pltpu
from jax.sharding import PartitionSpec as P

MESH = pl.DeviceIdType.MESH
F32 = jnp.float32
BF16 = jnp.bfloat16
ROWS = 1024
EMB = 1024
WIDTH = (5120, 1280)
LOCAL = (1280, 320)
PIECE = 128
HALF = 64
QUART = 32
NSEM = 160
NA, NB = 64, 64
CUT_A, CUT_B = 32, 32
IMAGE_A, IMAGE_B, TEXT_0, TEXT_1 = range(4)
KIND_A, KIND_B = 0, 1
MERGE = 2
(
    FIRST, FROM_LEFT, FROM_RIGHT, FINISH, STAGE_LOW, STAGE_HIGH, STAGE_FAR, PASS_LOW, PASS_HIGH, LAND,
    CAPTION_LOW, CAPTION_HIGH, CAPTION_FAR, SIBLING, TILE, POSITIVE,
) = range(16)
ORDER = [
    (FIRST, IMAGE_A),
    (FIRST, TEXT_0),
    (FIRST, IMAGE_B),
    (FIRST, TEXT_1),
    (FROM_RIGHT, IMAGE_A),
    (FROM_LEFT, IMAGE_A),
    (FROM_RIGHT, TEXT_0),
    (FROM_LEFT, TEXT_0),
    (FROM_LEFT, IMAGE_B),
    (FROM_RIGHT, IMAGE_B),
    (FROM_RIGHT, TEXT_1),
    (FROM_LEFT, TEXT_1),
    (FINISH, IMAGE_A),
    (FINISH, TEXT_0),
    (FINISH, IMAGE_B),
    (SIBLING, 0, 0),
    (FINISH, TEXT_1),
    (SIBLING, 1, 0),
    (PASS_LOW, KIND_A, 0),
    (STAGE_LOW, KIND_A),
    (CAPTION_LOW, 0, 1),
    (STAGE_HIGH, KIND_A),
    (CAPTION_HIGH, 0, 1),
    (SIBLING, 0, 1),
    (STAGE_LOW, KIND_B),
    (STAGE_HIGH, KIND_B),
    (CAPTION_HIGH, 1, 1),
    (PASS_LOW, KIND_B, 0),
    (CAPTION_LOW, 1, 1),
    (STAGE_FAR, KIND_A),
    (TILE, KIND_A, 0, (0,)),
    (CAPTION_LOW, 0, 2),
    (CAPTION_HIGH, 0, 2),
    (SIBLING, 0, -2),
    (PASS_LOW, KIND_B, -1),
    (PASS_HIGH, KIND_B, -1),
    (SIBLING, 1, -1),
    (SIBLING, 1, 1),
    (SIBLING, 0, -1),
    (PASS_HIGH, KIND_A, 0),
    (PASS_HIGH, KIND_B, 0),
    (SIBLING, 0, 2),
    (TILE, KIND_A, 0, (-1, 1)),
    (PASS_HIGH, KIND_A, 1),
    (CAPTION_LOW, 1, 2),
    (CAPTION_HIGH, 1, 2),
    (PASS_LOW, KIND_A, 1),
    (STAGE_FAR, KIND_B),
    (PASS_LOW, KIND_B, 1),
    (SIBLING, 1, 2),
    (PASS_HIGH, KIND_A, -1),
    (SIBLING, 1, -2),
    (PASS_LOW, KIND_A, -1),
    (PASS_HIGH, KIND_B, 1),
    (TILE, KIND_B, 0, (0, -1, 1, -2)),
    (TILE, KIND_A, 0, (-2, 2)),
    (CAPTION_HIGH, 0, 3),
    (TILE, KIND_B, 0, (2,)),
    (PASS_HIGH, KIND_A, 2),
    (CAPTION_LOW, 0, 3),
    (TILE, KIND_A, 1, (0, -1, 1, -2)),
    (PASS_LOW, KIND_A, 2),
    (TILE, KIND_A, -1, (0, -1, 1, -2)),
    (TILE, KIND_A, -1, (2,)),
    (TILE, KIND_A, 1, (2,)),
    (LAND, KIND_A, 1),
    (CAPTION_LOW, 1, 3),
    (LAND, KIND_B, -1),
    (CAPTION_HIGH, 1, 3),
    (PASS_LOW, KIND_B, 2),
    (LAND, KIND_A, 0),
    (PASS_HIGH, KIND_B, 2),
    (TILE, KIND_B, -1, (0, -1, 1, -2)),
    (CAPTION_FAR, 0),
    (SIBLING, 1, -3),
    (SIBLING, 0, -3),
    (SIBLING, 1, 3),
    (TILE, KIND_B, 1, (0, -1, 1, -2)),
    (TILE, KIND_B, -1, (2, -3)),
    (LAND, KIND_A, 2),
    (LAND, KIND_B, 1),
    (LAND, KIND_A, -1),
    (SIBLING, 0, 3),
    (LAND, KIND_B, 0),
    (POSITIVE,),
    (TILE, KIND_A, 2, (0, -1, 1, -2)),
    (LAND, KIND_B, 2),
    (SIBLING, 0, 4),
    (CAPTION_FAR, 1),
    (TILE, KIND_B, 2, (0, -1, 1, -2)),
    (SIBLING, 1, 4),
    (TILE, KIND_A, 2, (2, -3, 3, 4)),
    (TILE, KIND_B, 1, (2, -3, 3, 4)),
    (TILE, KIND_B, 2, (2, -3, 3, 4)),
    (TILE, KIND_A, 0, (-3, 3, 4)),
    (TILE, KIND_A, -1, (-3, 3, 4)),
    (TILE, KIND_A, 1, (-3, 3, 4)),
    (TILE, KIND_B, 0, (-3, 3, 4)),
    (TILE, KIND_B, -1, (3, 4)),
]
LOG2E = 1.4426950408889634
LN2 = 0.6931471805599453
LOW = -1e30


def wrap(value, count):
    return lax.rem(value + count, count)


def kernel(
    imf, txf, wim, wtx, scale_ref, pairs_ref, out,
    xi, xt, xtt, wi, wt, mus, pf, pb, misc_send, misc_recv, relay, comb, fin, turn, columns,
    img_a, img_b, txt, rmax_a, rsum_a, rmax_b, rsum_b, cmax, csum,
    rsend, rrecv, csend, crecv, fsend, frecv, lsem, ssem, rsem,
):
    tw = lax.axis_index("tower")
    blk = lax.axis_index("blk")
    x = lax.axis_index("mp")
    core = lax.rem(blk, 2)
    yh = lax.rem(blk // 2, 2)
    z = blk // 4
    y = yh * 2 + tw
    piece = tw * 4 + x

    def device(dx, dy, dz, dc):
        px = wrap(x + dx, 4)
        py = wrap(y + dy, 4)
        pz = wrap(z + dz, 8)
        pc = lax.rem(core + dc, 2)
        return {"tower": lax.rem(py, 2), "blk": (pz * 2 + py // 2) * 2 + pc, "mp": px}

    sent = []

    def send(src, dst, where):
        k = len(sent)
        copy = pltpu.make_async_remote_copy(
            src_ref=src, dst_ref=dst, send_sem=ssem.at[k], recv_sem=rsem.at[k],
            device_id=device(*where), device_id_type=MESH,
        )
        copy.start()
        sent.append(copy)
        return k

    def arrive(k, ref):
        pltpu.make_async_remote_copy(
            src_ref=ref, dst_ref=ref, send_sem=ssem.at[k], recv_sem=rsem.at[k],
            device_id=device(1, 0, 0, 0), device_id_type=MESH,
        ).wait_recv()

    half_rows = pl.ds(pl.multiple_of(tw * 512, 512), 512)
    loads = [
        pltpu.make_async_copy(imf.at[half_rows, :], xi, lsem.at[0]),
        pltpu.make_async_copy(wim, wi, lsem.at[1]),
        pltpu.make_async_copy(txf.at[:, half_rows], xt, lsem.at[2]),
        pltpu.make_async_copy(wtx, wt, lsem.at[3]),
    ]
    for load in loads:
        load.start()

    plane = [(dx, dy, 0, 0) for dy in range(4) for dx in range(4) if (dx, dy) != (0, 0)]
    column = [(0, 0, dz, dc) for dz in range(8) for dc in range(2) if (dz, dc) != (0, 0)]
    barrier = pltpu.get_barrier_semaphore()
    for to in plane + column:
        pl.semaphore_signal(barrier, inc=1, device_id=device(*to), device_id_type=MESH)

    lane = lax.broadcasted_iota(jnp.int32, (PIECE, PIECE), 1)

    def project(q, feats, weights):
        width = LOCAL[q]

        def rows_stats(d, carry):
            rows = pl.ds(pl.multiple_of(d * PIECE, PIECE), PIECE)
            if q == 0:
                values = feats[rows, :].astype(F32)
                first = jnp.sum(values, axis=1, keepdims=True)
                second = jnp.sum(values * values, axis=1, keepdims=True)
                mus[q, rows, :] = first / width
                flat = jnp.where(lane == 0, first, jnp.where(lane == 1, second, 0.0)).T
                first, second = flat[0:1, :], flat[1:2, :]
            else:
                values = feats[:, rows].astype(F32)
                first = jnp.sum(values, axis=0, keepdims=True)
                second = jnp.sum(values * values, axis=0, keepdims=True)
                flat = jnp.broadcast_to(first / width, (PIECE, PIECE)).T
                mus[q, rows, :] = flat[:, 0:1]
            misc_send[q, d, :, EMB : EMB + 128] = first
            misc_send[q, d, :, EMB + 128 : EMB + 256] = second
            return carry

        lax.fori_loop(0, 4, rows_stats, 0)
        lhs = feats
        if q == 1:
            lhs = xtt
            lhs[...] = feats[...].T

        def columns_step(n, carry):
            cols = pl.ds(pl.multiple_of(n * 256, 256), 256)
            block = weights[:, cols]
            total = jnp.dot(jnp.ones((8, width), BF16), block, preferred_element_type=F32)[0:1, :]
            part = jnp.dot(lhs[...], block, preferred_element_type=F32) - mus[q] * total
            pf[q, :, cols] = part
            pb[q, :, cols] = part.astype(BF16)
            for d in range(4):
                misc_send[q, d, :, cols] = total
            return carry

        lax.fori_loop(0, 4, columns_step, 0)

    right, left, opposite = wrap(x + 1, 4), wrap(x + 3, 4), wrap(x + 2, 4)

    def part_rows(owner, start, count):
        return pl.ds(pl.multiple_of(owner * PIECE + start, 16), count)

    def scatter_misc(q):
        return [send(misc_send.at[q, wrap(x + d, 4)], misc_recv.at[q, x], (d, 0, 0, 0)) for d in (1, 3, 2)]

    def scatter_first(q, start, count, cut):
        low, high = pl.ds(start, cut), pl.ds(start + cut, count - cut)
        return {
            "batch": (q, start, count, cut),
            "relay0": send(pb.at[q, part_rows(opposite, start, cut), :], relay.at[q, 0, low, :], (1, 0, 0, 0)),
            "relay1": send(
                pb.at[q, part_rows(opposite, start + cut, count - cut), :], relay.at[q, 1, high, :], (3, 0, 0, 0)
            ),
            "fin0b": send(
                pb.at[q, part_rows(right, start + cut, count - cut), :], fin.at[q, 0, high, :], (1, 0, 0, 0)
            ),
            "fin1a": send(pb.at[q, part_rows(left, start, cut), :], fin.at[q, 1, low, :], (3, 0, 0, 0)),
        }

    def settle(q, keys):
        for d, k in zip((1, 3, 2), keys):
            arrive(k, misc_recv.at[q, wrap(x - d, 4)])
        misc_recv[q, x] = misc_send[q, x]
        turn[...] = jnp.zeros_like(turn)
        first = [misc_recv[q, s, :, EMB : EMB + 128] for s in range(4)]
        second = [misc_recv[q, s, :, EMB + 128 : EMB + 256] for s in range(4)]
        mean = (first[0] + first[1] + first[2] + first[3]) / WIDTH[q]
        square = (second[0] + second[1] + second[2] + second[3]) / WIDTH[q]
        turn[4:5, :] = lax.rsqrt(square - mean * mean + 1e-06)
        for s in range(4):
            turn[s : s + 1, :] = first[s] / LOCAL[q] - mean
        columns[q] = turn[...].T

    def finish(keys):
        q, start, count, cut = keys["batch"]
        low, high, rows = pl.ds(start, cut), pl.ds(start + cut, count - cut), pl.ds(start, count)
        arrive(keys["fin0b"], fin.at[q, 0, high, :])
        arrive(keys["fin1a"], fin.at[q, 1, low, :])
        arrive(keys["fin0a"], fin.at[q, 0, low, :])
        arrive(keys["fin1b"], fin.at[q, 1, high, :])
        total = pf[q, part_rows(x, start, count), :] + fin[q, 0, rows, :].astype(F32) + fin[q, 1, rows, :].astype(F32)
        for s in range(4):
            total = total + columns[q, rows, s : s + 1] * misc_recv[q, s, :, 0:EMB]
        projected = total * columns[q, rows, 4:5]
        length = lax.rsqrt(jnp.sum(projected * projected, axis=1, keepdims=True) + 1e-06)
        return (projected * length).astype(BF16)

    def unit_a(dx, dy):
        return img_a, NA, wrap(y + dy, 4), wrap(x + dx, 4)

    def unit_b(dx, dy):
        return img_b, NB, wrap(x + dx, 4), wrap(y + dy, 4)

    CUT = {NA: CUT_A, NB: CUT_B}

    def chunk(where, part=None):
        ref, size, unit, place = where
        start, count = {None: (0, size), 0: (0, CUT[size]), 1: (CUT[size], size - CUT[size])}[part]
        return ref.at[unit, pl.ds(pl.multiple_of(place * size + start, 16), count), :]

    move = {"x": lambda s: (s, 0, 0, 0), "y": lambda s: (0, s, 0, 0)}

    def spread(axis, where):
        ref = chunk(where)
        return [send(ref, ref, move[axis](1)), send(ref, ref, move[axis](3))]

    def store_image(where, rows):
        ref, size, unit, place = where
        ref[unit, pl.ds(pl.multiple_of(place * size, 16), size), :] = rows

    def cap(dz, half, other=0, start=0, count=HALF):
        place = lax.rem(core + other, 2) * PIECE + half * HALF
        return txt.at[wrap(z + dz, 8), pl.ds(pl.multiple_of(place + start, 16), count), :]

    scale = scale_ref[0, 0]
    scale2 = scale * LOG2E

    def update(max_ref, sum_ref, unit, top, total):
        old, held = max_ref[unit], sum_ref[unit]
        gap = old - top
        small = jnp.exp2(-jnp.abs(gap))
        keep = gap >= 0
        max_ref[unit] = jnp.maximum(old, top)
        sum_ref[unit] = jnp.where(keep, held, total) + jnp.where(keep, total, held) * small

    def group(members, offsets):
        columns_of = [wrap(z + dz, 8) for dz in offsets]
        scores = [
            [
                scale2 * lax.dot_general(images[unit], txt[v], (((1,), (1,)), ((), ())), preferred_element_type=F32)
                for v in columns_of
            ]
            for images, max_ref, sum_ref, unit in members
        ]
        for i, v in enumerate(columns_of):
            top = jnp.max(scores[0][i], axis=0, keepdims=True)
            for row in scores[1:]:
                top = jnp.maximum(top, jnp.max(row[i], axis=0, keepdims=True))
            total = jnp.sum(jnp.exp2(scores[0][i] - top), axis=0, keepdims=True)
            for row in scores[1:]:
                total = total + jnp.sum(jnp.exp2(row[i] - top), axis=0, keepdims=True)
            update(cmax, csum, v, top, total)
        for row, (images, max_ref, sum_ref, unit) in zip(scores, members):
            widest = row[0]
            for block in row[1:]:
                widest = jnp.maximum(widest, block)
            top = jnp.max(widest, axis=1, keepdims=True)
            total = jnp.exp2(row[0] - top)
            for block in row[1:]:
                total = total + jnp.exp2(block - top)
            update(max_ref, sum_ref, unit, top, jnp.sum(total, axis=1, keepdims=True))

    def tile_run(items):
        merged = {}
        for _, kind, offset, offsets in items:
            if kind == KIND_A:
                member = (img_a, rmax_a, rsum_a, wrap(y + offset, 4))
            else:
                member = (img_b, rmax_b, rsum_b, wrap(x + offset, 4))
            merged.setdefault(offsets, []).append(member)
        for offsets, members in merged.items():
            for i in range(0, len(members), MERGE):
                group(members[i : i + MERGE], offsets)

    tasks = {}
    BATCH = {
        IMAGE_A: (0, 0, NA, CUT_A),
        IMAGE_B: (0, NA, NB, CUT_B),
        TEXT_0: (1, 0, HALF, QUART),
        TEXT_1: (1, HALF, HALF, QUART),
    }

    def start_batch(name):
        q, start, count, cut = BATCH[name]
        low, high = pl.ds(start, cut), pl.ds(start + cut, count - cut)
        keys = scatter_first(q, start, count, cut)

        def from_left():
            arrive(keys["relay0"], relay.at[q, 0, low, :])
            comb[q, low, :] = (
                pf[q, part_rows(right, start, cut), :] + relay[q, 0, low, :].astype(F32)
            ).astype(BF16)
            keys["fin0a"] = send(comb.at[q, low, :], fin.at[q, 0, low, :], (1, 0, 0, 0))

        def from_right():
            arrive(keys["relay1"], relay.at[q, 1, high, :])
            comb[q, high, :] = (
                pf[q, part_rows(left, start + cut, count - cut), :] + relay[q, 1, high, :].astype(F32)
            ).astype(BF16)
            keys["fin1b"] = send(comb.at[q, high, :], fin.at[q, 1, high, :], (3, 0, 0, 0))

        def last():
            if name in (IMAGE_A, TEXT_0):
                settle(q, misc_keys[q])
            rows = finish(keys)
            if name == IMAGE_A:
                store_image(unit_a(0, 0), rows)
                stage("x", KIND_A, spread("x", unit_a(0, 0)))
                second_stage("y", KIND_A, 0, spread("y", unit_a(0, 0)))
            elif name == IMAGE_B:
                store_image(unit_b(0, 0), rows)
                stage("y", KIND_B, spread("y", unit_b(0, 0)))
                second_stage("x", KIND_B, 0, spread("x", unit_b(0, 0)))
            else:
                half = name - TEXT_0
                txt[z, pl.ds(pl.multiple_of(core * PIECE + half * HALF, HALF), HALF), :] = rows
                ref = cap(0, half)
                low_key, high_key = send(ref, ref, (0, 0, 1, 0)), send(ref, ref, (0, 0, 7, 0))
                to_sibling(half, 0)
                captions(half, 1, low_key, high_key)

        tasks[FROM_LEFT, name] = from_left
        tasks[FROM_RIGHT, name] = from_right
        tasks[FINISH, name] = last

    def where(kind, along, across):
        return unit_a(along, across) if kind == KIND_A else unit_b(across, along)

    def stage(axis, kind, keys):
        other = "y" if axis == "x" else "x"
        far = {}

        def lower():
            ref = where(kind, -1, 0)
            arrive(keys[0], chunk(ref))
            far[0] = send(chunk(ref, 0), chunk(ref, 0), move[axis](1))
            second_stage(other, kind, -1, spread(other, ref))

        def upper():
            ref = where(kind, 1, 0)
            arrive(keys[1], chunk(ref))
            far[1] = send(chunk(ref, 1), chunk(ref, 1), move[axis](3))
            second_stage(other, kind, 1, spread(other, ref))

        def opposite_chunk():
            ref = where(kind, 2, 0)
            arrive(far[0], chunk(ref, 0))
            arrive(far[1], chunk(ref, 1))
            second_stage(other, kind, 2, spread(other, ref))

        tasks[STAGE_LOW, kind] = lower
        tasks[STAGE_HIGH, kind] = upper
        tasks[STAGE_FAR, kind] = opposite_chunk

    def second_stage(axis, kind, s, keys):
        far = {}

        def lower():
            ref = where(kind, s, -1)
            arrive(keys[0], chunk(ref))
            far[0] = send(chunk(ref, 0), chunk(ref, 0), move[axis](1))

        def upper():
            ref = where(kind, s, 1)
            arrive(keys[1], chunk(ref))
            far[1] = send(chunk(ref, 1), chunk(ref, 1), move[axis](3))

        def land():
            ref = where(kind, s, 2)
            arrive(far[0], chunk(ref, 0))
            arrive(far[1], chunk(ref, 1))

        tasks[PASS_LOW, kind, s] = lower
        tasks[PASS_HIGH, kind, s] = upper
        tasks[LAND, kind, s] = land

    def to_sibling(half, dz):
        key = send(cap(dz, half), cap(dz, half), (0, 0, 0, 1))
        tasks[SIBLING, half, dz] = lambda: arrive(key, cap(dz, half, 1))

    def captions(half, d, low_key, high_key):
        keys = {}

        def follow():
            if len(keys) < 2:
                return
            if d < 3:
                captions(half, d + 1, keys[0], keys[1])
                return

            def opposite_caption():
                arrive(keys[0], cap(4, half, 0, 0, QUART))
                arrive(keys[1], cap(4, half, 0, QUART, QUART))
                to_sibling(half, 4)

            tasks[CAPTION_FAR, half] = opposite_caption

        def lower():
            arrive(low_key, cap(-d, half))
            ref = cap(-d, half) if d < 3 else cap(-d, half, 0, 0, QUART)
            keys[0] = send(ref, ref, (0, 0, 1, 0))
            to_sibling(half, -d)
            follow()

        def upper():
            arrive(high_key, cap(d, half))
            ref = cap(d, half) if d < 3 else cap(d, half, 0, QUART, QUART)
            keys[1] = send(ref, ref, (0, 0, 7, 0))
            to_sibling(half, d)
            follow()

        tasks[CAPTION_LOW, half, d] = lower
        tasks[CAPTION_HIGH, half, d] = upper

    def positives():
        own_caps = txt[z, pl.ds(pl.multiple_of(core * PIECE, PIECE), PIECE), :]
        turn[...] = jnp.zeros_like(turn)
        turn[0:8, :] = pairs_ref[...].astype(F32)
        partner = turn[...].T
        mine = (piece * PIECE + lane).astype(F32)
        caption_positive = jnp.zeros((1, PIECE), F32)
        image_positive = jnp.zeros((PIECE, PIECE), F32)
        for p in range(8):
            t, px = p // 4, p % 4
            rows = jnp.concatenate(
                [
                    img_a[yh * 2 + t, px * NA : (px + 1) * NA, :],
                    img_b[px, pl.ds(pl.multiple_of((yh * 2 + t) * NB, 16), NB), :],
                ],
                axis=0,
            )
            scores = scale * lax.dot_general(
                rows, own_caps, (((1,), (1,)), ((), ())), preferred_element_type=F32
            )
            picked = jnp.where(partner[:, p : p + 1] == mine, scores, 0.0)
            caption_positive = caption_positive + jnp.sum(picked, axis=0, keepdims=True)
            image_positive = jnp.where(lane == p, jnp.sum(picked, axis=1, keepdims=True), image_positive)
        image_positive = image_positive.T

        return caption_positive, image_positive

    loads[0].wait()
    loads[1].wait()
    project(0, xi, wi)
    pl.semaphore_wait(barrier, len(plane) + len(column))
    misc_keys = {}
    run = []
    for item in ORDER + [None]:
        if item is not None and item[0] == TILE:
            run.append(item)
            continue
        tile_run(run)
        run = []
        if item is None:
            break
        if item[0] == POSITIVE:
            caption_positive, image_positive = positives()
        elif item[0] == FIRST:
            start_batch(item[1])
            if item[1] == IMAGE_A:
                misc_keys[0] = scatter_misc(0)
                loads[2].wait()
                loads[3].wait()
                project(1, xt, wt)
                misc_keys[1] = scatter_misc(1)
                for ref in (rmax_a, rmax_b, cmax):
                    ref[...] = jnp.full(ref.shape, LOW, F32)
                for ref in (rsum_a, rsum_b, csum):
                    ref[...] = jnp.zeros(ref.shape, F32)
        else:
            tasks.pop(item)()

    for u in range(8):
        logs = (cmax[u] + jnp.log2(csum[u])) * LN2
        csend[2 * u] = logs[:, 0:PIECE]
        csend[2 * u + 1] = logs[:, PIECE : 2 * PIECE]
    me_column = z * 2 + core
    column_keys = []
    for to in column:
        target = wrap(z + to[2], 8) * 2 + lax.rem(core + to[3], 2)
        column_keys.append(send(csend.at[target], crecv.at[me_column], to))

    def flat_logs(max_ref, sum_ref, size):
        wide = lax.broadcasted_iota(jnp.int32, (size, PIECE), 1)
        logs = jnp.zeros((size, PIECE), F32)
        for u in range(4):
            logs = jnp.where(wide == u, (max_ref[u] + jnp.log2(sum_ref[u])) * LN2, logs)
        padded = -(-size // PIECE) * PIECE
        if padded > size:
            logs = jnp.concatenate([logs, jnp.zeros((padded - size, PIECE), F32)], axis=0)
        return jnp.concatenate([logs[i : i + PIECE].T for i in range(0, padded, PIECE)], axis=1)

    flat_a = flat_logs(rmax_a, rsum_a, 4 * NA)
    flat_b = flat_logs(rmax_b, rsum_b, 4 * NB)
    same = [(yh == 0).astype(F32), (yh == 1).astype(F32)]
    for py in range(4):
        for px in range(4):
            rsend[py * 4 + px, 0:1, :] = jnp.concatenate(
                [flat_a[py : py + 1, px * NA : (px + 1) * NA], flat_b[px : px + 1, py * NB : (py + 1) * NB]], axis=1
            )
            p = (py % 2) * 4 + px
            rsend[py * 4 + px, 1:2, :] = image_positive[p : p + 1, :] * same[py // 2]
    me_plane = y * 4 + x
    plane_keys = []
    for to in plane:
        target = wrap(y + to[1], 4) * 4 + wrap(x + to[0], 4)
        plane_keys.append(send(rsend.at[target], rrecv.at[me_plane], to))
    crecv[me_column] = csend[me_column]
    rrecv[me_plane] = rsend[me_plane]
    early = len(sent) - len(column) - len(plane)
    for copy in sent[:early]:
        copy.wait_send()
    for to, k in zip(column, column_keys):
        source = wrap(z - to[2], 8) * 2 + lax.rem(core + to[3], 2)
        arrive(k, crecv.at[source])
    for to, k in zip(plane, plane_keys):
        source = wrap(y - to[1], 4) * 4 + wrap(x - to[0], 4)
        arrive(k, rrecv.at[source])

    def merge(rows):
        top = jnp.max(rows, axis=0)
        return top + jnp.log(jnp.sum(jnp.exp(rows - top[None]), axis=0))

    image_rows = rrecv[...]
    fsend[0:1, :] = merge(image_rows[:, 0:1, :]) - jnp.sum(image_rows[:, 1:2, :], axis=0)
    fsend[1:2, :] = merge(crecv[...]) - caption_positive
    shard = [(dx, dt) for dt in range(2) for dx in range(4) if (dx, dt) != (0, 0)]
    shard_keys = []
    step_y = [0, 1 - 2 * tw]
    for dx, dt in shard:
        shard_keys.append(send(fsend, frecv.at[piece], (dx, step_y[dt], 0, 0)))
    frecv[piece] = fsend[...]
    for (dx, dt), k in zip(shard, shard_keys):
        source = lax.rem(tw + dt, 2) * 4 + wrap(x - dx, 4)
        arrive(k, frecv.at[source])
    for p in range(8):
        out[p : p + 1, :] = frecv[p, 0:1, :]
        out[8 + p : 9 + p, :] = frecv[p, 1:2, :]
    for copy in sent[early:]:
        copy.wait_send()


def on_device(image_feats, text_feats, image_proj, text_proj, logit_scale, pairs):
    vmem = pl.BlockSpec(memory_space=pltpu.VMEM)
    hbm = pl.BlockSpec(memory_space=pl.ANY)
    losses = pl.pallas_call(
        kernel,
        out_shape=jax.ShapeDtypeStruct((16, 128), F32),
        in_specs=[hbm, hbm, hbm, hbm, pl.BlockSpec(memory_space=pltpu.SMEM), vmem],
        out_specs=vmem,
        scratch_shapes=[
            pltpu.VMEM((512, LOCAL[0]), BF16),
            pltpu.VMEM((LOCAL[1], 512), BF16),
            pltpu.VMEM((512, LOCAL[1]), BF16),
            pltpu.VMEM((LOCAL[0], EMB), BF16),
            pltpu.VMEM((LOCAL[1], EMB), BF16),
            pltpu.VMEM((2, 512, 1), F32),
            pltpu.VMEM((2, 512, EMB), F32),
            pltpu.VMEM((2, 512, EMB), BF16),
            pltpu.VMEM((2, 4, 1, EMB + 256), F32),
            pltpu.VMEM((2, 4, 1, EMB + 256), F32),
            pltpu.VMEM((2, 2, PIECE, EMB), BF16),
            pltpu.VMEM((2, PIECE, EMB), BF16),
            pltpu.VMEM((2, 2, PIECE, EMB), BF16),
            pltpu.VMEM((PIECE, PIECE), F32),
            pltpu.VMEM((2, PIECE, PIECE), F32),
            pltpu.VMEM((4, 4 * NA, EMB), BF16),
            pltpu.VMEM((4, 4 * NB, EMB), BF16),
            pltpu.VMEM((8, 256, EMB), BF16),
            pltpu.VMEM((4, 4 * NA, 1), F32),
            pltpu.VMEM((4, 4 * NA, 1), F32),
            pltpu.VMEM((4, 4 * NB, 1), F32),
            pltpu.VMEM((4, 4 * NB, 1), F32),
            pltpu.VMEM((8, 1, 256), F32),
            pltpu.VMEM((8, 1, 256), F32),
            pltpu.VMEM((16, 2, PIECE), F32),
            pltpu.VMEM((16, 2, PIECE), F32),
            pltpu.VMEM((16, 1, PIECE), F32),
            pltpu.VMEM((16, 1, PIECE), F32),
            pltpu.VMEM((2, PIECE), F32),
            pltpu.VMEM((8, 2, PIECE), F32),
            pltpu.SemaphoreType.DMA((4,)),
            pltpu.SemaphoreType.DMA((NSEM,)),
            pltpu.SemaphoreType.DMA((NSEM,)),
        ],
        compiler_params=pltpu.CompilerParams(
            collective_id=0, has_side_effects=True, vmem_limit_bytes=60 * 1024 * 1024
        ),
    )(
        image_feats, text_feats.T, image_proj, text_proj,
        logit_scale.reshape(1, 1), pairs.reshape(8, 128),
    )
    return (losses[0:8].reshape(ROWS), losses[8:16].reshape(ROWS))


def solution(mesh):
    return jax.shard_map(
        on_device,
        mesh=mesh,
        in_specs=(
            P("blk", "mp"),
            P("blk", "mp"),
            P("mp", None),
            P("mp", None),
            P(),
            P("blk", None),
        ),
        out_specs=(P("blk"), P("blk")),
        check_vma=False,
    )
```

```python
import jax
import jax.numpy as jnp
from jax import lax
from jax.experimental import pallas as pl
from jax.experimental.pallas import tpu as pltpu
from jax.sharding import PartitionSpec as P

MESH = pl.DeviceIdType.MESH
F32 = jnp.float32
BF16 = jnp.bfloat16
ROWS = 1024
EMB = 1024
WIDTH = (5120, 1280)
LOCAL = (1280, 320)
PIECE = 128
HALF = 64
QUART = 32
NSEM = 160
NA, NB = 64, 64
CUT_A, CUT_B = 32, 32
IMAGE_A, IMAGE_B, TEXT_0, TEXT_1 = range(4)
KIND_A, KIND_B = 0, 1
MERGE = 4
(
    FIRST, FROM_LEFT, FROM_RIGHT, FINISH, STAGE_LOW, STAGE_HIGH, STAGE_FAR, PASS_LOW, PASS_HIGH, LAND,
    CAPTION_LOW, CAPTION_HIGH, CAPTION_FAR, SIBLING, TILE, POSITIVE,
) = range(16)
ORDER = [
    (FIRST, IMAGE_A),
    (FIRST, TEXT_0),
    (FIRST, IMAGE_B),
    (FIRST, TEXT_1),
    (FROM_RIGHT, IMAGE_A),
    (FROM_LEFT, IMAGE_A),
    (FROM_RIGHT, TEXT_0),
    (FROM_LEFT, TEXT_0),
    (FROM_LEFT, IMAGE_B),
    (FROM_RIGHT, IMAGE_B),
    (FROM_RIGHT, TEXT_1),
    (FROM_LEFT, TEXT_1),
    (FINISH, IMAGE_A),
    (FINISH, TEXT_0),
    (FINISH, IMAGE_B),
    (SIBLING, 0, 0),
    (FINISH, TEXT_1),
    (SIBLING, 1, 0),
    (PASS_LOW, KIND_A, 0),
    (STAGE_LOW, KIND_A),
    (CAPTION_LOW, 0, 1),
    (STAGE_HIGH, KIND_A),
    (CAPTION_HIGH, 0, 1),
    (SIBLING, 0, 1),
    (STAGE_LOW, KIND_B),
    (STAGE_HIGH, KIND_B),
    (CAPTION_HIGH, 1, 1),
    (PASS_LOW, KIND_B, 0),
    (CAPTION_LOW, 1, 1),
    (STAGE_FAR, KIND_A),
    (TILE, KIND_A, 0, (0,)),
    (CAPTION_LOW, 0, 2),
    (CAPTION_HIGH, 0, 2),
    (SIBLING, 0, -2),
    (PASS_LOW, KIND_B, -1),
    (PASS_HIGH, KIND_B, -1),
    (SIBLING, 1, -1),
    (SIBLING, 1, 1),
    (SIBLING, 0, -1),
    (PASS_HIGH, KIND_A, 0),
    (PASS_HIGH, KIND_B, 0),
    (SIBLING, 0, 2),
    (TILE, KIND_A, 0, (-1, 1)),
    (PASS_HIGH, KIND_A, 1),
    (CAPTION_LOW, 1, 2),
    (CAPTION_HIGH, 1, 2),
    (PASS_LOW, KIND_A, 1),
    (STAGE_FAR, KIND_B),
    (PASS_LOW, KIND_B, 1),
    (SIBLING, 1, 2),
    (PASS_HIGH, KIND_A, -1),
    (SIBLING, 1, -2),
    (PASS_LOW, KIND_A, -1),
    (PASS_HIGH, KIND_B, 1),
    (TILE, KIND_B, 0, (0, -1, 1, -2)),
    (TILE, KIND_A, 0, (-2, 2)),
    (CAPTION_HIGH, 0, 3),
    (TILE, KIND_B, 0, (2,)),
    (PASS_HIGH, KIND_A, 2),
    (CAPTION_LOW, 0, 3),
    (TILE, KIND_A, 1, (0, -1, 1, -2)),
    (PASS_LOW, KIND_A, 2),
    (TILE, KIND_A, -1, (0, -1, 1, -2)),
    (TILE, KIND_A, -1, (2,)),
    (TILE, KIND_A, 1, (2,)),
    (LAND, KIND_A, 1),
    (CAPTION_LOW, 1, 3),
    (LAND, KIND_B, -1),
    (CAPTION_HIGH, 1, 3),
    (PASS_LOW, KIND_B, 2),
    (LAND, KIND_A, 0),
    (PASS_HIGH, KIND_B, 2),
    (TILE, KIND_B, -1, (0, -1, 1, -2)),
    (CAPTION_FAR, 0),
    (SIBLING, 1, -3),
    (SIBLING, 0, -3),
    (SIBLING, 1, 3),
    (TILE, KIND_B, 1, (0, -1, 1, -2)),
    (TILE, KIND_B, -1, (2, -3)),
    (LAND, KIND_A, 2),
    (LAND, KIND_B, 1),
    (LAND, KIND_A, -1),
    (SIBLING, 0, 3),
    (LAND, KIND_B, 0),
    (POSITIVE,),
    (TILE, KIND_A, 2, (0, -1, 1, -2)),
    (LAND, KIND_B, 2),
    (SIBLING, 0, 4),
    (CAPTION_FAR, 1),
    (TILE, KIND_B, 2, (0, -1, 1, -2)),
    (SIBLING, 1, 4),
    (TILE, KIND_A, 2, (2, -3, 3, 4)),
    (TILE, KIND_B, 1, (2, -3, 3, 4)),
    (TILE, KIND_B, 2, (2, -3, 3, 4)),
    (TILE, KIND_A, 0, (-3, 3, 4)),
    (TILE, KIND_A, -1, (-3, 3, 4)),
    (TILE, KIND_A, 1, (-3, 3, 4)),
    (TILE, KIND_B, 0, (-3, 3, 4)),
    (TILE, KIND_B, -1, (3, 4)),
]
LOG2E = 1.4426950408889634
LN2 = 0.6931471805599453
LOW = -1e30


def wrap(value, count):
    return lax.rem(value + count, count)


def kernel(
    imf, txf, wim, wtx, scale_ref, pairs_ref, out,
    xi, xt, xtt, wi, wt, mus, pf, pb, misc_send, misc_recv, relay, comb, fin, turn, columns,
    img_a, img_b, txt, rmax_a, rsum_a, rmax_b, rsum_b, cmax, csum,
    rsend, rrecv, csend, crecv, fsend, frecv, lsem, ssem, rsem,
):
    tw = lax.axis_index("tower")
    blk = lax.axis_index("blk")
    x = lax.axis_index("mp")
    core = lax.rem(blk, 2)
    yh = lax.rem(blk // 2, 2)
    z = blk // 4
    y = yh * 2 + tw
    piece = tw * 4 + x

    def device(dx, dy, dz, dc):
        px = wrap(x + dx, 4)
        py = wrap(y + dy, 4)
        pz = wrap(z + dz, 8)
        pc = lax.rem(core + dc, 2)
        return {"tower": lax.rem(py, 2), "blk": (pz * 2 + py // 2) * 2 + pc, "mp": px}

    sent = []

    def send(src, dst, where):
        k = len(sent)
        copy = pltpu.make_async_remote_copy(
            src_ref=src, dst_ref=dst, send_sem=ssem.at[k], recv_sem=rsem.at[k],
            device_id=device(*where), device_id_type=MESH,
        )
        copy.start()
        sent.append(copy)
        return k

    def arrive(k, ref):
        pltpu.make_async_remote_copy(
            src_ref=ref, dst_ref=ref, send_sem=ssem.at[k], recv_sem=rsem.at[k],
            device_id=device(1, 0, 0, 0), device_id_type=MESH,
        ).wait_recv()

    half_rows = pl.ds(pl.multiple_of(tw * 512, 512), 512)
    loads = [
        pltpu.make_async_copy(imf.at[half_rows, :], xi, lsem.at[0]),
        pltpu.make_async_copy(wim, wi, lsem.at[1]),
        pltpu.make_async_copy(txf.at[:, half_rows], xt, lsem.at[2]),
        pltpu.make_async_copy(wtx, wt, lsem.at[3]),
    ]
    for load in loads:
        load.start()

    plane = [(dx, dy, 0, 0) for dy in range(4) for dx in range(4) if (dx, dy) != (0, 0)]
    column = [(0, 0, dz, dc) for dz in range(8) for dc in range(2) if (dz, dc) != (0, 0)]
    barrier = pltpu.get_barrier_semaphore()
    for to in plane + column:
        pl.semaphore_signal(barrier, inc=1, device_id=device(*to), device_id_type=MESH)

    lane = lax.broadcasted_iota(jnp.int32, (PIECE, PIECE), 1)

    def project(q, feats, weights):
        width = LOCAL[q]

        def rows_stats(d, carry):
            rows = pl.ds(pl.multiple_of(d * PIECE, PIECE), PIECE)
            if q == 0:
                values = feats[rows, :].astype(F32)
                first = jnp.sum(values, axis=1, keepdims=True)
                second = jnp.sum(values * values, axis=1, keepdims=True)
                mus[q, rows, :] = first / width
                flat = jnp.where(lane == 0, first, jnp.where(lane == 1, second, 0.0)).T
                first, second = flat[0:1, :], flat[1:2, :]
            else:
                values = feats[:, rows].astype(F32)
                first = jnp.sum(values, axis=0, keepdims=True)
                second = jnp.sum(values * values, axis=0, keepdims=True)
                flat = jnp.broadcast_to(first / width, (PIECE, PIECE)).T
                mus[q, rows, :] = flat[:, 0:1]
            misc_send[q, d, :, EMB : EMB + 128] = first
            misc_send[q, d, :, EMB + 128 : EMB + 256] = second
            return carry

        lax.fori_loop(0, 4, rows_stats, 0)
        lhs = feats
        if q == 1:
            lhs = xtt
            lhs[...] = feats[...].T

        def columns_step(n, carry):
            cols = pl.ds(pl.multiple_of(n * 256, 256), 256)
            block = weights[:, cols]
            total = jnp.dot(jnp.ones((8, width), BF16), block, preferred_element_type=F32)[0:1, :]
            part = jnp.dot(lhs[...], block, preferred_element_type=F32) - mus[q] * total
            pf[q, :, cols] = part
            pb[q, :, cols] = part.astype(BF16)
            for d in range(4):
                misc_send[q, d, :, cols] = total
            return carry

        lax.fori_loop(0, 4, columns_step, 0)

    right, left, opposite = wrap(x + 1, 4), wrap(x + 3, 4), wrap(x + 2, 4)

    def part_rows(owner, start, count):
        return pl.ds(pl.multiple_of(owner * PIECE + start, 16), count)

    def scatter_misc(q):
        return [send(misc_send.at[q, wrap(x + d, 4)], misc_recv.at[q, x], (d, 0, 0, 0)) for d in (1, 3, 2)]

    def scatter_first(q, start, count, cut):
        low, high = pl.ds(start, cut), pl.ds(start + cut, count - cut)
        return {
            "batch": (q, start, count, cut),
            "relay0": send(pb.at[q, part_rows(opposite, start, cut), :], relay.at[q, 0, low, :], (1, 0, 0, 0)),
            "relay1": send(
                pb.at[q, part_rows(opposite, start + cut, count - cut), :], relay.at[q, 1, high, :], (3, 0, 0, 0)
            ),
            "fin0b": send(
                pb.at[q, part_rows(right, start + cut, count - cut), :], fin.at[q, 0, high, :], (1, 0, 0, 0)
            ),
            "fin1a": send(pb.at[q, part_rows(left, start, cut), :], fin.at[q, 1, low, :], (3, 0, 0, 0)),
        }

    def settle(q, keys):
        for d, k in zip((1, 3, 2), keys):
            arrive(k, misc_recv.at[q, wrap(x - d, 4)])
        misc_recv[q, x] = misc_send[q, x]
        turn[...] = jnp.zeros_like(turn)
        first = [misc_recv[q, s, :, EMB : EMB + 128] for s in range(4)]
        second = [misc_recv[q, s, :, EMB + 128 : EMB + 256] for s in range(4)]
        mean = (first[0] + first[1] + first[2] + first[3]) / WIDTH[q]
        square = (second[0] + second[1] + second[2] + second[3]) / WIDTH[q]
        turn[4:5, :] = lax.rsqrt(square - mean * mean + 1e-06)
        for s in range(4):
            turn[s : s + 1, :] = first[s] / LOCAL[q] - mean
        columns[q] = turn[...].T

    def finish(keys):
        q, start, count, cut = keys["batch"]
        low, high, rows = pl.ds(start, cut), pl.ds(start + cut, count - cut), pl.ds(start, count)
        arrive(keys["fin0b"], fin.at[q, 0, high, :])
        arrive(keys["fin1a"], fin.at[q, 1, low, :])
        arrive(keys["fin0a"], fin.at[q, 0, low, :])
        arrive(keys["fin1b"], fin.at[q, 1, high, :])
        total = pf[q, part_rows(x, start, count), :] + fin[q, 0, rows, :].astype(F32) + fin[q, 1, rows, :].astype(F32)
        for s in range(4):
            total = total + columns[q, rows, s : s + 1] * misc_recv[q, s, :, 0:EMB]
        projected = total * columns[q, rows, 4:5]
        length = lax.rsqrt(jnp.sum(projected * projected, axis=1, keepdims=True) + 1e-06)
        return (projected * length).astype(BF16)

    def unit_a(dx, dy):
        return img_a, NA, wrap(y + dy, 4), wrap(x + dx, 4)

    def unit_b(dx, dy):
        return img_b, NB, wrap(x + dx, 4), wrap(y + dy, 4)

    CUT = {NA: CUT_A, NB: CUT_B}

    def chunk(where, part=None):
        ref, size, unit, place = where
        start, count = {None: (0, size), 0: (0, CUT[size]), 1: (CUT[size], size - CUT[size])}[part]
        return ref.at[unit, pl.ds(pl.multiple_of(place * size + start, 16), count), :]

    move = {"x": lambda s: (s, 0, 0, 0), "y": lambda s: (0, s, 0, 0)}

    def spread(axis, where):
        ref = chunk(where)
        return [send(ref, ref, move[axis](1)), send(ref, ref, move[axis](3))]

    def store_image(where, rows):
        ref, size, unit, place = where
        ref[unit, pl.ds(pl.multiple_of(place * size, 16), size), :] = rows

    def cap(dz, half, other=0, start=0, count=HALF):
        place = lax.rem(core + other, 2) * PIECE + half * HALF
        return txt.at[wrap(z + dz, 8), pl.ds(pl.multiple_of(place + start, 16), count), :]

    scale = scale_ref[0, 0]
    scale2 = scale * LOG2E

    def update(max_ref, sum_ref, unit, top, total):
        old, held = max_ref[unit], sum_ref[unit]
        gap = old - top
        small = jnp.exp2(-jnp.abs(gap))
        keep = gap >= 0
        max_ref[unit] = jnp.maximum(old, top)
        sum_ref[unit] = jnp.where(keep, held, total) + jnp.where(keep, total, held) * small

    def group(members, offsets):
        columns_of = [wrap(z + dz, 8) for dz in offsets]
        scores = [
            [
                scale2 * lax.dot_general(images[unit], txt[v], (((1,), (1,)), ((), ())), preferred_element_type=F32)
                for v in columns_of
            ]
            for images, max_ref, sum_ref, unit in members
        ]
        for i, v in enumerate(columns_of):
            top = jnp.max(scores[0][i], axis=0, keepdims=True)
            for row in scores[1:]:
                top = jnp.maximum(top, jnp.max(row[i], axis=0, keepdims=True))
            total = jnp.sum(jnp.exp2(scores[0][i] - top), axis=0, keepdims=True)
            for row in scores[1:]:
                total = total + jnp.sum(jnp.exp2(row[i] - top), axis=0, keepdims=True)
            update(cmax, csum, v, top, total)
        for row, (images, max_ref, sum_ref, unit) in zip(scores, members):
            widest = row[0]
            for block in row[1:]:
                widest = jnp.maximum(widest, block)
            top = jnp.max(widest, axis=1, keepdims=True)
            total = jnp.exp2(row[0] - top)
            for block in row[1:]:
                total = total + jnp.exp2(block - top)
            update(max_ref, sum_ref, unit, top, jnp.sum(total, axis=1, keepdims=True))

    def tile_run(items):
        merged = {}
        for _, kind, offset, offsets in items:
            if kind == KIND_A:
                member = (img_a, rmax_a, rsum_a, wrap(y + offset, 4))
            else:
                member = (img_b, rmax_b, rsum_b, wrap(x + offset, 4))
            merged.setdefault(offsets, []).append(member)
        for offsets, members in merged.items():
            for i in range(0, len(members), MERGE):
                group(members[i : i + MERGE], offsets)

    tasks = {}
    BATCH = {
        IMAGE_A: (0, 0, NA, CUT_A),
        IMAGE_B: (0, NA, NB, CUT_B),
        TEXT_0: (1, 0, HALF, QUART),
        TEXT_1: (1, HALF, HALF, QUART),
    }

    def start_batch(name):
        q, start, count, cut = BATCH[name]
        low, high = pl.ds(start, cut), pl.ds(start + cut, count - cut)
        keys = scatter_first(q, start, count, cut)

        def from_left():
            arrive(keys["relay0"], relay.at[q, 0, low, :])
            comb[q, low, :] = (
                pf[q, part_rows(right, start, cut), :] + relay[q, 0, low, :].astype(F32)
            ).astype(BF16)
            keys["fin0a"] = send(comb.at[q, low, :], fin.at[q, 0, low, :], (1, 0, 0, 0))

        def from_right():
            arrive(keys["relay1"], relay.at[q, 1, high, :])
            comb[q, high, :] = (
                pf[q, part_rows(left, start + cut, count - cut), :] + relay[q, 1, high, :].astype(F32)
            ).astype(BF16)
            keys["fin1b"] = send(comb.at[q, high, :], fin.at[q, 1, high, :], (3, 0, 0, 0))

        def last():
            if name in (IMAGE_A, TEXT_0):
                settle(q, misc_keys[q])
            rows = finish(keys)
            if name == IMAGE_A:
                store_image(unit_a(0, 0), rows)
                stage("x", KIND_A, spread("x", unit_a(0, 0)))
                second_stage("y", KIND_A, 0, spread("y", unit_a(0, 0)))
            elif name == IMAGE_B:
                store_image(unit_b(0, 0), rows)
                stage("y", KIND_B, spread("y", unit_b(0, 0)))
                second_stage("x", KIND_B, 0, spread("x", unit_b(0, 0)))
            else:
                half = name - TEXT_0
                txt[z, pl.ds(pl.multiple_of(core * PIECE + half * HALF, HALF), HALF), :] = rows
                ref = cap(0, half)
                low_key, high_key = send(ref, ref, (0, 0, 1, 0)), send(ref, ref, (0, 0, 7, 0))
                to_sibling(half, 0)
                captions(half, 1, low_key, high_key)

        tasks[FROM_LEFT, name] = from_left
        tasks[FROM_RIGHT, name] = from_right
        tasks[FINISH, name] = last

    def where(kind, along, across):
        return unit_a(along, across) if kind == KIND_A else unit_b(across, along)

    def stage(axis, kind, keys):
        other = "y" if axis == "x" else "x"
        far = {}

        def lower():
            ref = where(kind, -1, 0)
            arrive(keys[0], chunk(ref))
            far[0] = send(chunk(ref, 0), chunk(ref, 0), move[axis](1))
            second_stage(other, kind, -1, spread(other, ref))

        def upper():
            ref = where(kind, 1, 0)
            arrive(keys[1], chunk(ref))
            far[1] = send(chunk(ref, 1), chunk(ref, 1), move[axis](3))
            second_stage(other, kind, 1, spread(other, ref))

        def opposite_chunk():
            ref = where(kind, 2, 0)
            arrive(far[0], chunk(ref, 0))
            arrive(far[1], chunk(ref, 1))
            second_stage(other, kind, 2, spread(other, ref))

        tasks[STAGE_LOW, kind] = lower
        tasks[STAGE_HIGH, kind] = upper
        tasks[STAGE_FAR, kind] = opposite_chunk

    def second_stage(axis, kind, s, keys):
        far = {}

        def lower():
            ref = where(kind, s, -1)
            arrive(keys[0], chunk(ref))
            far[0] = send(chunk(ref, 0), chunk(ref, 0), move[axis](1))

        def upper():
            ref = where(kind, s, 1)
            arrive(keys[1], chunk(ref))
            far[1] = send(chunk(ref, 1), chunk(ref, 1), move[axis](3))

        def land():
            ref = where(kind, s, 2)
            arrive(far[0], chunk(ref, 0))
            arrive(far[1], chunk(ref, 1))

        tasks[PASS_LOW, kind, s] = lower
        tasks[PASS_HIGH, kind, s] = upper
        tasks[LAND, kind, s] = land

    def to_sibling(half, dz):
        key = send(cap(dz, half), cap(dz, half), (0, 0, 0, 1))
        tasks[SIBLING, half, dz] = lambda: arrive(key, cap(dz, half, 1))

    def captions(half, d, low_key, high_key):
        keys = {}

        def follow():
            if len(keys) < 2:
                return
            if d < 3:
                captions(half, d + 1, keys[0], keys[1])
                return

            def opposite_caption():
                arrive(keys[0], cap(4, half, 0, 0, QUART))
                arrive(keys[1], cap(4, half, 0, QUART, QUART))
                to_sibling(half, 4)

            tasks[CAPTION_FAR, half] = opposite_caption

        def lower():
            arrive(low_key, cap(-d, half))
            ref = cap(-d, half) if d < 3 else cap(-d, half, 0, 0, QUART)
            keys[0] = send(ref, ref, (0, 0, 1, 0))
            to_sibling(half, -d)
            follow()

        def upper():
            arrive(high_key, cap(d, half))
            ref = cap(d, half) if d < 3 else cap(d, half, 0, QUART, QUART)
            keys[1] = send(ref, ref, (0, 0, 7, 0))
            to_sibling(half, d)
            follow()

        tasks[CAPTION_LOW, half, d] = lower
        tasks[CAPTION_HIGH, half, d] = upper

    def positives():
        own_caps = txt[z, pl.ds(pl.multiple_of(core * PIECE, PIECE), PIECE), :]
        turn[...] = jnp.zeros_like(turn)
        turn[0:8, :] = pairs_ref[...].astype(F32)
        partner = turn[...].T
        mine = (piece * PIECE + lane).astype(F32)
        caption_positive = jnp.zeros((1, PIECE), F32)
        image_positive = jnp.zeros((PIECE, PIECE), F32)
        for p in range(8):
            t, px = p // 4, p % 4
            rows = jnp.concatenate(
                [
                    img_a[yh * 2 + t, px * NA : (px + 1) * NA, :],
                    img_b[px, pl.ds(pl.multiple_of((yh * 2 + t) * NB, 16), NB), :],
                ],
                axis=0,
            )
            scores = scale * lax.dot_general(
                rows, own_caps, (((1,), (1,)), ((), ())), preferred_element_type=F32
            )
            picked = jnp.where(partner[:, p : p + 1] == mine, scores, 0.0)
            caption_positive = caption_positive + jnp.sum(picked, axis=0, keepdims=True)
            image_positive = jnp.where(lane == p, jnp.sum(picked, axis=1, keepdims=True), image_positive)
        image_positive = image_positive.T

        return caption_positive, image_positive

    loads[0].wait()
    loads[1].wait()
    project(0, xi, wi)
    pl.semaphore_wait(barrier, len(plane) + len(column))
    misc_keys = {}
    run = []
    for item in ORDER + [None]:
        if item is not None and item[0] == TILE:
            run.append(item)
            continue
        tile_run(run)
        run = []
        if item is None:
            break
        if item[0] == POSITIVE:
            caption_positive, image_positive = positives()
        elif item[0] == FIRST:
            start_batch(item[1])
            if item[1] == IMAGE_A:
                misc_keys[0] = scatter_misc(0)
                loads[2].wait()
                loads[3].wait()
                project(1, xt, wt)
                misc_keys[1] = scatter_misc(1)
                for ref in (rmax_a, rmax_b, cmax):
                    ref[...] = jnp.full(ref.shape, LOW, F32)
                for ref in (rsum_a, rsum_b, csum):
                    ref[...] = jnp.zeros(ref.shape, F32)
        else:
            tasks.pop(item)()

    for u in range(8):
        logs = (cmax[u] + jnp.log2(csum[u])) * LN2
        csend[2 * u] = logs[:, 0:PIECE]
        csend[2 * u + 1] = logs[:, PIECE : 2 * PIECE]
    me_column = z * 2 + core
    column_keys = []
    for to in column:
        target = wrap(z + to[2], 8) * 2 + lax.rem(core + to[3], 2)
        column_keys.append(send(csend.at[target], crecv.at[me_column], to))

    def flat_logs(max_ref, sum_ref, size):
        wide = lax.broadcasted_iota(jnp.int32, (size, PIECE), 1)
        logs = jnp.zeros((size, PIECE), F32)
        for u in range(4):
            logs = jnp.where(wide == u, (max_ref[u] + jnp.log2(sum_ref[u])) * LN2, logs)
        padded = -(-size // PIECE) * PIECE
        if padded > size:
            logs = jnp.concatenate([logs, jnp.zeros((padded - size, PIECE), F32)], axis=0)
        return jnp.concatenate([logs[i : i + PIECE].T for i in range(0, padded, PIECE)], axis=1)

    flat_a = flat_logs(rmax_a, rsum_a, 4 * NA)
    flat_b = flat_logs(rmax_b, rsum_b, 4 * NB)
    same = [(yh == 0).astype(F32), (yh == 1).astype(F32)]
    for py in range(4):
        for px in range(4):
            rsend[py * 4 + px, 0:1, :] = jnp.concatenate(
                [flat_a[py : py + 1, px * NA : (px + 1) * NA], flat_b[px : px + 1, py * NB : (py + 1) * NB]], axis=1
            )
            p = (py % 2) * 4 + px
            rsend[py * 4 + px, 1:2, :] = image_positive[p : p + 1, :] * same[py // 2]
    me_plane = y * 4 + x
    plane_keys = []
    for to in plane:
        target = wrap(y + to[1], 4) * 4 + wrap(x + to[0], 4)
        plane_keys.append(send(rsend.at[target], rrecv.at[me_plane], to))
    crecv[me_column] = csend[me_column]
    rrecv[me_plane] = rsend[me_plane]
    early = len(sent) - len(column) - len(plane)
    for copy in sent[:early]:
        copy.wait_send()
    for to, k in zip(column, column_keys):
        source = wrap(z - to[2], 8) * 2 + lax.rem(core + to[3], 2)
        arrive(k, crecv.at[source])
    for to, k in zip(plane, plane_keys):
        source = wrap(y - to[1], 4) * 4 + wrap(x - to[0], 4)
        arrive(k, rrecv.at[source])

    def merge(rows):
        top = jnp.max(rows, axis=0)
        return top + jnp.log(jnp.sum(jnp.exp(rows - top[None]), axis=0))

    image_rows = rrecv[...]
    fsend[0:1, :] = merge(image_rows[:, 0:1, :]) - jnp.sum(image_rows[:, 1:2, :], axis=0)
    fsend[1:2, :] = merge(crecv[...]) - caption_positive
    shard = [(dx, dt) for dt in range(2) for dx in range(4) if (dx, dt) != (0, 0)]
    shard_keys = []
    step_y = [0, 1 - 2 * tw]
    for dx, dt in shard:
        shard_keys.append(send(fsend, frecv.at[piece], (dx, step_y[dt], 0, 0)))
    frecv[piece] = fsend[...]
    for (dx, dt), k in zip(shard, shard_keys):
        source = lax.rem(tw + dt, 2) * 4 + wrap(x - dx, 4)
        arrive(k, frecv.at[source])
    for p in range(8):
        out[p : p + 1, :] = frecv[p, 0:1, :]
        out[8 + p : 9 + p, :] = frecv[p, 1:2, :]
    for copy in sent[early:]:
        copy.wait_send()


def on_device(image_feats, text_feats, image_proj, text_proj, logit_scale, pairs):
    vmem = pl.BlockSpec(memory_space=pltpu.VMEM)
    hbm = pl.BlockSpec(memory_space=pl.ANY)
    losses = pl.pallas_call(
        kernel,
        out_shape=jax.ShapeDtypeStruct((16, 128), F32),
        in_specs=[hbm, hbm, hbm, hbm, pl.BlockSpec(memory_space=pltpu.SMEM), vmem],
        out_specs=vmem,
        scratch_shapes=[
            pltpu.VMEM((512, LOCAL[0]), BF16),
            pltpu.VMEM((LOCAL[1], 512), BF16),
            pltpu.VMEM((512, LOCAL[1]), BF16),
            pltpu.VMEM((LOCAL[0], EMB), BF16),
            pltpu.VMEM((LOCAL[1], EMB), BF16),
            pltpu.VMEM((2, 512, 1), F32),
            pltpu.VMEM((2, 512, EMB), F32),
            pltpu.VMEM((2, 512, EMB), BF16),
            pltpu.VMEM((2, 4, 1, EMB + 256), F32),
            pltpu.VMEM((2, 4, 1, EMB + 256), F32),
            pltpu.VMEM((2, 2, PIECE, EMB), BF16),
            pltpu.VMEM((2, PIECE, EMB), BF16),
            pltpu.VMEM((2, 2, PIECE, EMB), BF16),
            pltpu.VMEM((PIECE, PIECE), F32),
            pltpu.VMEM((2, PIECE, PIECE), F32),
            pltpu.VMEM((4, 4 * NA, EMB), BF16),
            pltpu.VMEM((4, 4 * NB, EMB), BF16),
            pltpu.VMEM((8, 256, EMB), BF16),
            pltpu.VMEM((4, 4 * NA, 1), F32),
            pltpu.VMEM((4, 4 * NA, 1), F32),
            pltpu.VMEM((4, 4 * NB, 1), F32),
            pltpu.VMEM((4, 4 * NB, 1), F32),
            pltpu.VMEM((8, 1, 256), F32),
            pltpu.VMEM((8, 1, 256), F32),
            pltpu.VMEM((16, 2, PIECE), F32),
            pltpu.VMEM((16, 2, PIECE), F32),
            pltpu.VMEM((16, 1, PIECE), F32),
            pltpu.VMEM((16, 1, PIECE), F32),
            pltpu.VMEM((2, PIECE), F32),
            pltpu.VMEM((8, 2, PIECE), F32),
            pltpu.SemaphoreType.DMA((4,)),
            pltpu.SemaphoreType.DMA((NSEM,)),
            pltpu.SemaphoreType.DMA((NSEM,)),
        ],
        compiler_params=pltpu.CompilerParams(
            collective_id=0, has_side_effects=True, vmem_limit_bytes=60 * 1024 * 1024
        ),
    )(
        image_feats, text_feats.T, image_proj, text_proj,
        logit_scale.reshape(1, 1), pairs.reshape(8, 128),
    )
    return (losses[0:8].reshape(ROWS), losses[8:16].reshape(ROWS))


def solution(mesh):
    return jax.shard_map(
        on_device,
        mesh=mesh,
        in_specs=(
            P("blk", "mp"),
            P("blk", "mp"),
            P("mp", None),
            P("mp", None),
            P(),
            P("blk", None),
        ),
        out_specs=(P("blk"), P("blk")),
        check_vma=False,
    )
```
